32 devices in a mesh: grp: 4 (over x, core), blk: 8 (over z, y).
Axes of the slice: x: 2, y: 2, z: 4, core: 2. Of those that a mesh axis runs over, the one named last changes fastest.
Arguments:
- pair_density: bfloat16 [2048, 8192], P('grp', 'blk'), may hold values from -14 to 14
- energies: float32 [2048], P('grp'), may hold values from 1 to 4
- batch_live: int32 [4], replicated, may hold values from 1 to 512, 1280 in all
- coulomb_root: float32 [8192], replicated, may hold values from 0.5 to 2
Outputs:
- polarized: bfloat16 [4, 8192, 8192], P('grp', 'blk')
- screened: float32 [4, 8192, 128], P('grp', 'blk')
The draws below stay inside these ranges and needn't reach their ends.
Inputs may be any that keep to these rules, and one draw needn't show every extreme that they name: Group g's live transitions are its first batch_live[g] slots of 512; at least one group is full.
All inputs are finite; a program needn't handle non-finite values.
Results may differ from the reference program's by a relative error of at most 0.03.
Values may be sent and summed in bfloat16 or wider, within the bound.
A program may use at most 128 MiB of HBM per device.

```python
import math
import jax
import jax.numpy as jnp
import numpy as np

G = 8192
T_GRP = 512
CW = 128
DYSON = 2
TRANS = 2048
GROUPS = 4


def steps_of(own_key, extent, cuts, smallest, largest):
    gain, own = 1.0, jax.random.fold_in(own_key, 6)
    for position, parts in cuts:
        heights = jnp.exp(jax.random.uniform(jax.random.fold_in(own, position), (parts,), jnp.float32, smallest / len(cuts), largest / len(cuts)))
        gain = gain * jnp.repeat(heights, extent[position] // parts).reshape([-1 if axis == position else 1 for axis in range(len(extent))])
    return gain


def split_up(count, total, bound, skew):
    weights = [(1 << 20) // math.isqrt(rank ** skew) + 1 for rank in range(2, count + 1)]
    spare, counts = total - bound - (count - 1), [1] * (count - 1)
    while spare > 0:
        free = [i for i in range(count - 1) if counts[i] < bound]
        mass, budget = sum([weights[i] for i in free]), spare
        for i in free:
            more = min(bound - counts[i], max(1, budget * weights[i] // mass), spare)
            counts[i] = counts[i] + more
            spare = spare - more
    return np.array([bound] + counts)


def uneven(rng, amount, total, most, slope):
    if amount == 2:
        one = jax.random.randint(rng, (), max(1, total - most), min(most, total - 1) + 1)
        return jnp.stack([one, total - one])
    sizes = jnp.asarray(split_up(amount, total, most, slope), jnp.int32)
    pairs = (amount - 1) // 2
    giver, taker = sizes[1:1 + 2 * pairs:2], sizes[2:2 + 2 * pairs:2]
    room = jnp.minimum(giver - 1, most - taker)
    passed = jax.random.randint(jax.random.fold_in(rng, 1), (pairs,), 0, 1 << 20) % (room + 1)
    sizes = sizes.at[1:1 + 2 * pairs:2].set(giver - passed).at[2:2 + 2 * pairs:2].set(taker + passed)
    return sizes[jax.random.permutation(jax.random.fold_in(rng, 2), amount)]


def gaussian(stream_key, dims, deviation, most, pieces=(), held_as=jnp.bfloat16):
    array = jax.random.normal(stream_key, dims, jnp.float32) * deviation
    if len(pieces) > 0:
        array = steps_of(stream_key, dims, pieces, -0.22, 0.18) * array
    return jnp.clip(array, min=-most, max=most).astype(held_as)


def setup_inputs(seed: int = 0) -> dict:
    seeds = jax.random.split(jax.random.key(seed), 5)
    pair_density = gaussian(seeds[0], (TRANS, G), 3.0, 14.0, ((0, 4), (1, 8)))
    energies = jnp.clip(jnp.exp(math.log(4.0) - 1.3862944 * jax.random.uniform(seeds[1], (TRANS,), jnp.float32) ** steps_of(seeds[1], (TRANS,), ((0, 4),), -0.2, 0.2)), 1.0, 4.0)
    batch_live = uneven(seeds[2], GROUPS, 5 * T_GRP // 2, T_GRP, 2).astype(jnp.int32)
    coulomb_root = jnp.clip(jnp.exp(jax.random.uniform(seeds[3], (G,), jnp.float32, math.log(0.5), math.log(2.0))), 0.5, 2.0)
    return dict(pair_density=pair_density, energies=energies, batch_live=batch_live, coulomb_root=coulomb_root)


def reference(pair_density, energies, batch_live, coulomb_root):
    positions = jnp.arange(TRANS, dtype=jnp.int32)
    limits = batch_live[positions // T_GRP]
    is_live = (positions % T_GRP < limits).astype(jnp.float32)
    norm_factor = 1.0 / math.sqrt(TRANS)
    dense = pair_density.astype(jnp.float32)
    polar_list = []
    screen_list = []
    for freq_index in range(GROUPS):
        frequency = 0.6 * freq_index
        weight = -2.0 * energies / (energies * energies + frequency * frequency) * is_live * norm_factor
        scaled = (weight[:, None] * dense).astype(jnp.bfloat16)
        chi = jnp.dot(scaled.T, pair_density, preferred_element_type=jnp.float32)
        tiles = coulomb_root[:, None] * chi * coulomb_root[None, :]
        polarized = tiles.astype(jnp.bfloat16)
        window = tiles[:, :CW]
        state = window
        for dyson_step in range(DYSON):
            product = jnp.dot(polarized, state.astype(jnp.bfloat16), preferred_element_type=jnp.float32)
            state = window + 8.0 / G * product
        polar_list.append(polarized)
        screen_list.append(state)
    return (jnp.stack(polar_list), jnp.stack(screen_list))
```

```python
import functools
import math

import jax
import jax.numpy as jnp
from jax import lax
from jax.experimental import pallas as pl
from jax.experimental.pallas import tpu as pltpu
from jax.sharding import PartitionSpec as P

G = 8192
CW = 128
DYSON = 2
LANES = 128


def live_weights(all_energy, batch_live, slots, total_slots, group_ids, frequencies, norm_factor):
    positions = jnp.arange(total_slots, dtype=jnp.int32)
    owner_match = (positions // slots)[:, None] == group_ids[None, :]
    limits = jnp.sum(jnp.where(owner_match, batch_live[None, :], 0), axis=1)
    is_live = (positions % slots < limits).astype(jnp.float32)
    weight = (
        -2.0
        * all_energy[None, :]
        / (all_energy[None, :] * all_energy[None, :] + frequencies[:, None] * frequencies[:, None])
    )
    return weight * is_live[None, :] * norm_factor


def plain_body(pair_density, energies, batch_live, coulomb_root):
    slots = pair_density.shape[0]
    width_own = pair_density.shape[1]
    group_count = lax.axis_size("grp")
    block_count = lax.axis_size("blk")
    total_slots = slots * group_count
    group_index = lax.axis_index("grp")
    block_index = lax.axis_index("blk")
    norm_factor = 1.0 / math.sqrt(total_slots)
    own_root = lax.dynamic_slice_in_dim(coulomb_root, block_index * width_own, width_own)
    group_ids = jnp.arange(group_count, dtype=jnp.int32)
    row_density, all_energy = (
        lax.all_gather(pair_density, "grp", axis=0, tiled=True),
        lax.all_gather(energies.astype(jnp.bfloat16), "grp", axis=0, tiled=True).astype(
            energies.dtype
        ),
    )
    frequencies = 0.6 * jnp.arange(group_count, dtype=jnp.float32)
    weight = live_weights(
        all_energy, batch_live, slots, total_slots, group_ids, frequencies, norm_factor
    )
    scaled = (weight[:, :, None] * row_density.astype(jnp.float32)[None, :, :]).astype(jnp.bfloat16)
    sub_width = width_own // group_count
    my_slice = lax.dynamic_slice_in_dim(row_density, group_index * sub_width, sub_width, 1)
    root_table = jnp.reshape(coulomb_root, (block_count, group_count, sub_width))
    my_roots = jnp.reshape(
        lax.dynamic_index_in_dim(root_table, group_index, 1, keepdims=False), (-1,)
    )
    chi = jnp.einsum(
        "ftc,tk->fck",
        scaled,
        lax.all_gather(my_slice, "blk", axis=1, tiled=True),
        preferred_element_type=jnp.float32,
    )
    quarter = own_root[None, :, None] * chi * my_roots[None, None, :]
    received = lax.all_to_all(
        quarter.astype(jnp.bfloat16), "grp", split_axis=0, concat_axis=0, tiled=True
    )
    received = jnp.reshape(received, (group_count, width_own, block_count, sub_width))
    polarized = jnp.reshape(
        jnp.transpose(received, (1, 2, 0, 3)), (width_own, width_own * block_count)
    )
    lead_blocks = (CW + width_own - 1) // width_own
    lead = quarter[:, :, : lead_blocks * sub_width]
    lead_back = lax.all_to_all(
        lead.astype(jnp.bfloat16), "grp", split_axis=0, concat_axis=0, tiled=True
    ).astype(lead.dtype)
    lead_back = jnp.reshape(lead_back, (group_count, width_own, lead_blocks, sub_width))
    window = jnp.reshape(
        jnp.transpose(lead_back, (1, 2, 0, 3)), (width_own, lead_blocks * width_own)
    )[:, :CW]
    state = window
    for dyson_step in range(DYSON):
        rounded = state.astype(jnp.bfloat16)
        product = jnp.dot(
            polarized,
            lax.all_gather(rounded, "blk", axis=0, tiled=True),
            preferred_element_type=jnp.float32,
        )
        state = window + 8.0 / G * product
    return (polarized[None], state[None])


def pack_rows(batch_live, slots, total, packed):
    ends = jnp.cumsum(batch_live)
    starts = ends - batch_live
    j = jnp.arange(packed, dtype=jnp.int32)
    in_group = (j[:, None] >= starts[None, :]) & (j[:, None] < ends[None, :])
    group_base = jnp.arange(batch_live.shape[0], dtype=jnp.int32) * slots - starts
    source = jnp.sum(jnp.where(in_group, group_base[None, :] + j[:, None], 0), axis=1)
    used = jnp.any(in_group, axis=1)
    source = jnp.where(used, source, -1)
    return source, used


def chi_kernel(n, factor, a_ref, p_ref, w_ref, r_ref, out_ref, s_ref, at_ref, q_ref, u_ref, v_ref):
    i = pl.program_id(0)
    width = a_ref.shape[0]
    last = (((1,), (1,)), ((), ()))
    piece = p_ref[0, 0]
    root = r_ref[...]

    @pl.when(i == 0)
    def _():
        at_ref[:width] = a_ref[...]
        lead = p_ref[0, 0, :, :CW].astype(jnp.float32) * root[:, :CW]
        q = lead.T
        q_ref[...] = q
        at_ref[width:] = (q * w_ref[...]).astype(jnp.bfloat16)
        u_ref[...] = jnp.zeros_like(u_ref)

    @pl.when(i < n)
    def _():
        prod = jnp.dot(at_ref[...], piece, preferred_element_type=jnp.float32) * root
        out_ref[...] = prod[:width].astype(jnp.bfloat16)
        u_ref[...] += lax.dot_general(
            (prod[width:] * root).astype(jnp.bfloat16), piece, last,
            preferred_element_type=jnp.float32)

    @pl.when(i == n - 1)
    def _():
        v_ref[...] = (u_ref[...] * (w_ref[...] * factor)).astype(jnp.bfloat16)

    @pl.when(i >= n)
    def _():
        prod = jnp.dot(v_ref[...], piece, preferred_element_type=jnp.float32)
        u_ref[...] += lax.dot_general(
            (prod * (root * root)).astype(jnp.bfloat16), piece, last,
            preferred_element_type=jnp.float32)

    @pl.when(i == 2 * n - 1)
    def _():
        x = (q_ref[...] + factor * u_ref[...]).astype(jnp.bfloat16)
        s_ref[...] = lax.dot_general(a_ref[...], x, last, preferred_element_type=jnp.float32)


def chi_and_screen(left, pieces, weight, coulomb_root):
    width, packed = left.shape
    split, blocks, _, sub = pieces.shape
    n = split * blocks
    return pl.pallas_call(
        functools.partial(chi_kernel, n, 8.0 / G),
        grid=(2 * n,),
        out_shape=(
            jax.ShapeDtypeStruct((width, n * sub), jnp.bfloat16),
            jax.ShapeDtypeStruct((width, CW), jnp.float32),
        ),
        in_specs=[
            pl.BlockSpec((width, packed), lambda i: (0, 0)),
            pl.BlockSpec((1, 1, packed, sub), lambda i: (i % split, (i // split) % blocks, 0, 0)),
            pl.BlockSpec((1, packed), lambda i: (0, 0)),
            pl.BlockSpec((1, sub), lambda i: (0, i % n)),
        ],
        out_specs=(
            pl.BlockSpec((width, sub), lambda i: (0, jnp.minimum(i, n - 1))),
            pl.BlockSpec((width, CW), lambda i: (0, 0)),
        ),
        scratch_shapes=[
            pltpu.VMEM((width + CW, packed), jnp.bfloat16),
            pltpu.VMEM((CW, packed), jnp.float32),
            pltpu.VMEM((CW, packed), jnp.float32),
            pltpu.VMEM((CW, packed), jnp.bfloat16),
        ],
        compiler_params=pltpu.CompilerParams(vmem_limit_bytes=48 * 1024 * 1024),
    )(left, pieces, weight[None, :], coulomb_root[None, :])


def gather_pieces(own, group_index, group_count, blocks):
    sub = own.shape[1] // group_count
    mine = lax.dynamic_slice_in_dim(own, group_index * sub, sub, 1)
    row = lax.all_gather(mine, "blk", axis=0, tiled=False)
    return lax.all_gather(row, "grp", axis=0, tiled=False)


def body(pair_density, energies, batch_live, coulomb_root):
    slots, width = pair_density.shape
    group_count = lax.axis_size("grp")
    blocks = lax.axis_size("blk")
    total = slots * group_count
    packed = total * 5 // 8
    group_index = lax.axis_index("grp")
    block_index = lax.axis_index("blk")
    own_root = lax.dynamic_slice_in_dim(coulomb_root, block_index * width, width)

    rows = lax.all_gather(pair_density, "grp", axis=0, tiled=True)
    all_energy = lax.all_gather(energies, "grp", axis=0, tiled=True)
    source, used = pack_rows(batch_live, slots, total, packed)
    pick = source[:, None] == jnp.arange(total, dtype=jnp.int32)[None, :]
    own = jnp.dot(pick.astype(jnp.bfloat16), rows, preferred_element_type=jnp.float32).astype(
        jnp.bfloat16
    )
    energy = jnp.sum(jnp.where(pick, all_energy[None, :], 0.0), axis=1)
    energy = jnp.where(used, energy, 1.0)
    frequency = 0.6 * group_index.astype(jnp.float32)
    weight = -2.0 * energy / (energy * energy + frequency * frequency)
    weight = jnp.where(used, weight, 0.0) * (1.0 / math.sqrt(total))
    left = (own.T.astype(jnp.float32) * weight[None, :] * own_root[:, None]).astype(jnp.bfloat16)
    pieces = gather_pieces(own, group_index, group_count, blocks)
    polarized, screened = chi_and_screen(left, pieces, weight, coulomb_root)
    return (polarized[None], screened[None])


def solution(mesh):
    placed = (P("grp", "blk"), P("grp"), P(), P())
    aligned = (G // mesh.shape["blk"]) % (LANES * mesh.shape["grp"]) == 0
    return jax.shard_map(
        body if aligned else plain_body,
        mesh=mesh,
        in_specs=placed,
        out_specs=(P("grp", "blk", None), P("grp", "blk", None)),
        check_vma=False,
    )
```

```python
import functools
import math

import jax
import jax.numpy as jnp
from jax import lax
from jax.experimental import pallas as pl
from jax.experimental.pallas import tpu as pltpu
from jax.sharding import PartitionSpec as P

G = 8192
CW = 128
DYSON = 2
LANES = 128


def live_weights(all_energy, batch_live, slots, total_slots, group_ids, frequencies, norm_factor):
    positions = jnp.arange(total_slots, dtype=jnp.int32)
    owner_match = (positions // slots)[:, None] == group_ids[None, :]
    limits = jnp.sum(jnp.where(owner_match, batch_live[None, :], 0), axis=1)
    is_live = (positions % slots < limits).astype(jnp.float32)
    weight = (
        -2.0
        * all_energy[None, :]
        / (all_energy[None, :] * all_energy[None, :] + frequencies[:, None] * frequencies[:, None])
    )
    return weight * is_live[None, :] * norm_factor


def plain_body(pair_density, energies, batch_live, coulomb_root):
    slots = pair_density.shape[0]
    width_own = pair_density.shape[1]
    group_count = lax.axis_size("grp")
    block_count = lax.axis_size("blk")
    total_slots = slots * group_count
    group_index = lax.axis_index("grp")
    block_index = lax.axis_index("blk")
    norm_factor = 1.0 / math.sqrt(total_slots)
    own_root = lax.dynamic_slice_in_dim(coulomb_root, block_index * width_own, width_own)
    group_ids = jnp.arange(group_count, dtype=jnp.int32)
    row_density, all_energy = (
        lax.all_gather(pair_density, "grp", axis=0, tiled=True),
        lax.all_gather(energies.astype(jnp.bfloat16), "grp", axis=0, tiled=True).astype(
            energies.dtype
        ),
    )
    frequencies = 0.6 * jnp.arange(group_count, dtype=jnp.float32)
    weight = live_weights(
        all_energy, batch_live, slots, total_slots, group_ids, frequencies, norm_factor
    )
    scaled = (weight[:, :, None] * row_density.astype(jnp.float32)[None, :, :]).astype(jnp.bfloat16)
    sub_width = width_own // group_count
    my_slice = lax.dynamic_slice_in_dim(row_density, group_index * sub_width, sub_width, 1)
    root_table = jnp.reshape(coulomb_root, (block_count, group_count, sub_width))
    my_roots = jnp.reshape(
        lax.dynamic_index_in_dim(root_table, group_index, 1, keepdims=False), (-1,)
    )
    chi = jnp.einsum(
        "ftc,tk->fck",
        scaled,
        lax.all_gather(my_slice, "blk", axis=1, tiled=True),
        preferred_element_type=jnp.float32,
    )
    quarter = own_root[None, :, None] * chi * my_roots[None, None, :]
    received = lax.all_to_all(
        quarter.astype(jnp.bfloat16), "grp", split_axis=0, concat_axis=0, tiled=True
    )
    received = jnp.reshape(received, (group_count, width_own, block_count, sub_width))
    polarized = jnp.reshape(
        jnp.transpose(received, (1, 2, 0, 3)), (width_own, width_own * block_count)
    )
    lead_blocks = (CW + width_own - 1) // width_own
    lead = quarter[:, :, : lead_blocks * sub_width]
    lead_back = lax.all_to_all(
        lead.astype(jnp.bfloat16), "grp", split_axis=0, concat_axis=0, tiled=True
    ).astype(lead.dtype)
    lead_back = jnp.reshape(lead_back, (group_count, width_own, lead_blocks, sub_width))
    window = jnp.reshape(
        jnp.transpose(lead_back, (1, 2, 0, 3)), (width_own, lead_blocks * width_own)
    )[:, :CW]
    state = window
    for dyson_step in range(DYSON):
        rounded = state.astype(jnp.bfloat16)
        product = jnp.dot(
            polarized,
            lax.all_gather(rounded, "blk", axis=0, tiled=True),
            preferred_element_type=jnp.float32,
        )
        state = window + 8.0 / G * product
    return (polarized[None], state[None])


def pack_rows(batch_live, slots, total, packed):
    ends = jnp.cumsum(batch_live)
    starts = ends - batch_live
    j = jnp.arange(packed, dtype=jnp.int32)
    in_group = (j[:, None] >= starts[None, :]) & (j[:, None] < ends[None, :])
    group_base = jnp.arange(batch_live.shape[0], dtype=jnp.int32) * slots - starts
    source = jnp.sum(jnp.where(in_group, group_base[None, :] + j[:, None], 0), axis=1)
    used = jnp.any(in_group, axis=1)
    source = jnp.where(used, source, -1)
    return source, used


def chi_kernel(n, factor, a_ref, p_ref, w_ref, r_ref, out_ref, s_ref, at_ref, q_ref, u_ref, v_ref):
    i = pl.program_id(0)
    width = a_ref.shape[0]
    last = (((1,), (1,)), ((), ()))
    piece = p_ref[0, 0]
    root = r_ref[...]

    @pl.when(i == 0)
    def _():
        at_ref[:width] = a_ref[...]
        lead = p_ref[0, 0, :, :CW].astype(jnp.float32) * root[:, :CW]
        q = lead.T
        q_ref[...] = q
        at_ref[width:] = (q * w_ref[...]).astype(jnp.bfloat16)
        u_ref[...] = jnp.zeros_like(u_ref)

    @pl.when(i < n)
    def _():
        prod = jnp.dot(at_ref[...], piece, preferred_element_type=jnp.float32) * root
        out_ref[...] = prod[:width].astype(jnp.bfloat16)
        u_ref[...] += lax.dot_general(
            (prod[width:] * root).astype(jnp.bfloat16), piece, last,
            preferred_element_type=jnp.float32)

    @pl.when(i == n - 1)
    def _():
        v_ref[...] = (u_ref[...] * (w_ref[...] * factor)).astype(jnp.bfloat16)

    @pl.when(i >= n)
    def _():
        prod = jnp.dot(v_ref[...], piece, preferred_element_type=jnp.float32)
        u_ref[...] += lax.dot_general(
            (prod * (root * root)).astype(jnp.bfloat16), piece, last,
            preferred_element_type=jnp.float32)

    @pl.when(i == 2 * n - 1)
    def _():
        x = (q_ref[...] + factor * u_ref[...]).astype(jnp.bfloat16)
        s_ref[...] = lax.dot_general(a_ref[...], x, last, preferred_element_type=jnp.float32)


def chi_and_screen(left, pieces, weight, coulomb_root):
    width, packed = left.shape
    split, blocks, _, sub = pieces.shape
    n = split * blocks
    return pl.pallas_call(
        functools.partial(chi_kernel, n, 8.0 / G),
        grid=(2 * n,),
        out_shape=(
            jax.ShapeDtypeStruct((width, n * sub), jnp.bfloat16),
            jax.ShapeDtypeStruct((width, CW), jnp.float32),
        ),
        in_specs=[
            pl.BlockSpec((width, packed), lambda i: (0, 0)),
            pl.BlockSpec((1, 1, packed, sub), lambda i: (i % split, (i // split) % blocks, 0, 0)),
            pl.BlockSpec((1, packed), lambda i: (0, 0)),
            pl.BlockSpec((1, sub), lambda i: (0, i % n)),
        ],
        out_specs=(
            pl.BlockSpec((width, sub), lambda i: (0, jnp.minimum(i, n - 1))),
            pl.BlockSpec((width, CW), lambda i: (0, 0)),
        ),
        scratch_shapes=[
            pltpu.VMEM((width + CW, packed), jnp.bfloat16),
            pltpu.VMEM((CW, packed), jnp.float32),
            pltpu.VMEM((CW, packed), jnp.float32),
            pltpu.VMEM((CW, packed), jnp.bfloat16),
        ],
        compiler_params=pltpu.CompilerParams(vmem_limit_bytes=48 * 1024 * 1024),
    )(left, pieces, weight[None, :], coulomb_root[None, :])


def gather_kernel(nz, own_ref, out_ref, recv, s_up, s_down, s_y, s_x, s_pair, s_own):
    g, b = lax.axis_index("grp"), lax.axis_index("blk")
    x, c = g // 2, g % 2
    z, y = b // 2, b % 2
    half = own_ref.shape[1] // 2
    rows = pl.ds(pl.multiple_of(c * half, half), half)
    other_rows = pl.ds(pl.multiple_of((1 - c) * half, half), half)
    to_up, to_down = (g, b + 2), (g, b - 2)
    to_y = (g, z * 2 + 1 - y)
    to_x = ((1 - x) * 2 + c, b)
    to_pair = (x * 2 + 1 - c, b)
    has_up, has_down = z + 1 < nz, z >= 1
    skip_y, own_x = 2 * (1 - x), 2 * x

    def copy(q, bb, sem, to, own=False):
        src = own_ref.at[q, rows] if own else out_ref.at[q, bb, rows]
        return pltpu.make_async_remote_copy(
            src_ref=src, dst_ref=out_ref.at[q, bb, rows], send_sem=sem,
            recv_sem=recv.at[q, bb, c], device_id=to, device_id_type=pl.DeviceIdType.MESH)

    def arrived(q, bb):
        copy(q, bb, s_pair.at[q, bb], to_pair).wait_recv()

    def up(zz, j, own=False):
        return copy(x + j, zz * 2 + y, s_up.at[j, zz], to_up, own)

    def down(zz, j, own=False):
        return copy(x + j, zz * 2 + y, s_down.at[j, zz], to_down, own)

    def over_y(zz, j, own=False):
        return copy(x + j, zz * 2 + y, s_y.at[j, zz], to_y, own)

    def over_x(zz, yy, j):
        return copy(x + j, zz * 2 + yy, s_x.at[j, zz * 2 + yy], to_x)

    def over_pair(q, bb):
        return copy(q, bb, s_pair.at[q, bb], to_pair)

    def takes_y(zz, j):
        return (zz % 2 == 0) | (j != skip_y)

    def other_y_takes_x(zz, j):
        return ((zz % 2 == 0) & (j == own_x)) | ((zz % 2 == 1) & (j != skip_y))

    def when(condition, make, act):
        @pl.when(condition)
        def _():
            getattr(make(), act)()

    def from_z(zz, j, below, valid):
        @pl.when(valid)
        def _():
            q, bb = x + j, zz * 2 + y
            arrived(q, bb)
            if below:
                when(has_up, lambda: up(zz, j), "start")
            else:
                when(has_down, lambda: down(zz, j), "start")
            when(takes_y(zz, j), lambda: over_y(zz, j), "start")
            when(j == own_x, lambda: over_x(zz, y, j), "start")
            over_pair(q, bb).start()

    def from_y(zz, j, valid):
        @pl.when(valid & takes_y(zz, j))
        def _():
            q, bb = x + j, zz * 2 + 1 - y
            arrived(q, bb)
            when(other_y_takes_x(zz, j), lambda: over_x(zz, 1 - y, j), "start")
            over_pair(q, bb).start()

    def from_x(zz, same_y, valid):
        bb = zz * 2 + (y if same_y else 1 - y)

        def take(q):
            arrived(q, bb)
            over_pair(q, bb).start()

        if same_y:
            @pl.when(valid)
            def _():
                take(3 * (1 - x))
        else:
            @pl.when(valid & (zz % 2 == 0))
            def _():
                take(3 * (1 - x))

            @pl.when(valid & (zz % 2 == 1))
            def _():
                take(2 * (1 - x))
                take(2 * (1 - x) + 1)

    def at_distance(d):
        if d == 0:
            return [(z, True, z >= 0)]
        return [(z - d, True, z >= d), (z + d, False, z + d < nz)]

    barrier = pltpu.get_barrier_semaphore()

    def greet(to):
        pl.semaphore_signal(barrier, inc=1, device_id=to, device_id_type=pl.DeviceIdType.MESH)

    for to in (to_y, to_x, to_pair):
        greet(to)
    pl.when(has_up)(lambda: greet(to_up))
    pl.when(has_down)(lambda: greet(to_down))
    peers = 3 + has_up.astype(jnp.int32) + has_down.astype(jnp.int32)
    pl.semaphore_wait(barrier, peers)

    for j in range(3):
        when(has_up, lambda: up(z, j, True), "start")
        when(has_down, lambda: down(z, j, True), "start")
        when(takes_y(z, j), lambda: over_y(z, j, True), "start")
    keep = pltpu.make_async_copy(own_ref, out_ref.at[:, b], s_own)
    keep.start()

    for s in range(nz + 1):
        for j in range(3):
            if 1 <= s + 1 < nz:
                for zz, below, valid in at_distance(s + 1):
                    from_z(zz, j, below, valid)
            if s < nz:
                for zz, _, valid in at_distance(s):
                    from_y(zz, j, valid)
        if 1 <= s < nz:
            for zz, _, valid in at_distance(s):
                from_x(zz, True, valid)
        if s >= 1:
            for zz, _, valid in at_distance(s - 1):
                from_x(zz, False, valid)

    def from_pair(q, bb):
        pltpu.make_async_remote_copy(
            src_ref=out_ref.at[q, bb, other_rows], dst_ref=out_ref.at[q, bb, other_rows],
            send_sem=s_pair.at[q, bb], recv_sem=recv.at[q, bb, 1 - c],
            device_id=to_pair, device_id_type=pl.DeviceIdType.MESH).wait_recv()
        over_pair(q, bb).wait_send()

    keep.wait()
    for j in range(3):
        when(has_up, lambda: up(z, j, True), "wait_send")
        when(has_down, lambda: down(z, j, True), "wait_send")
        when(takes_y(z, j), lambda: over_y(z, j, True), "wait_send")
    for d in range(nz):
        for zz, below, valid in at_distance(d):
            for j in range(3):
                if d >= 1:
                    if below:
                        when(valid & has_up, lambda: up(zz, j), "wait_send")
                    else:
                        when(valid & has_down, lambda: down(zz, j), "wait_send")
                    when(valid & takes_y(zz, j), lambda: over_y(zz, j), "wait_send")
                    when(valid & (j == own_x), lambda: over_x(zz, y, j), "wait_send")
                when(valid & other_y_takes_x(zz, j), lambda: over_x(zz, 1 - y, j), "wait_send")
            for same_y in (True, False):
                if d >= 1 or not same_y:
                    for q in range(4):
                        pl.when(valid)(
                            lambda q=q: from_pair(q, zz * 2 + (y if same_y else 1 - y)))


def gather_pieces(own, blocks):
    split, packed, sub = own.shape
    nz = blocks // 2
    dma = pltpu.SemaphoreType.DMA
    sent = 28 * packed * sub
    return pl.pallas_call(
        functools.partial(gather_kernel, nz),
        out_shape=jax.ShapeDtypeStruct((split, blocks, packed, sub), own.dtype),
        in_specs=[pl.BlockSpec(memory_space=pltpu.VMEM)],
        out_specs=pl.BlockSpec(memory_space=pl.ANY),
        scratch_shapes=[
            dma((split, blocks, 2)), dma((3, nz)), dma((3, nz)), dma((3, nz)),
            dma((3, blocks)), dma((split, blocks)), dma(()),
        ],
        compiler_params=pltpu.CompilerParams(collective_id=0, has_side_effects=True),
        cost_estimate=pl.CostEstimate(flops=0, bytes_accessed=2 * sent, transcendentals=0),
    )(own)


def body(pair_density, energies, batch_live, coulomb_root):
    slots, width = pair_density.shape
    group_count = lax.axis_size("grp")
    blocks = lax.axis_size("blk")
    total = slots * group_count
    packed = total * 5 // 8
    group_index = lax.axis_index("grp")
    block_index = lax.axis_index("blk")
    own_root = lax.dynamic_slice_in_dim(coulomb_root, block_index * width, width)

    rows = lax.all_gather(pair_density, "grp", axis=0, tiled=True)
    all_energy = lax.all_gather(energies, "grp", axis=0, tiled=True)
    source, used = pack_rows(batch_live, slots, total, packed)
    pick = source[:, None] == jnp.arange(total, dtype=jnp.int32)[None, :]
    own = jnp.dot(pick.astype(jnp.bfloat16), rows, preferred_element_type=jnp.float32).astype(
        jnp.bfloat16
    )
    energy = jnp.sum(jnp.where(pick, all_energy[None, :], 0.0), axis=1)
    energy = jnp.where(used, energy, 1.0)
    frequency = 0.6 * group_index.astype(jnp.float32)
    weight = -2.0 * energy / (energy * energy + frequency * frequency)
    weight = jnp.where(used, weight, 0.0) * (1.0 / math.sqrt(total))
    left = (own.T.astype(jnp.float32) * weight[None, :] * own_root[:, None]).astype(jnp.bfloat16)
    quarters = jnp.transpose(
        jnp.reshape(own, (packed, group_count, width // group_count)), (1, 0, 2))
    pieces = gather_pieces(quarters, blocks)
    polarized, screened = chi_and_screen(left, pieces, weight, coulomb_root)
    return (polarized[None], screened[None])


def solution(mesh):
    placed = (P("grp", "blk"), P("grp"), P(), P())
    aligned = (
        mesh.shape["grp"] == 4
        and mesh.shape["blk"] % 2 == 0
        and (G // mesh.shape["blk"]) % (LANES * mesh.shape["grp"]) == 0
    )
    return jax.shard_map(
        body if aligned else plain_body,
        mesh=mesh,
        in_specs=placed,
        out_specs=(P("grp", "blk", None), P("grp", "blk", None)),
        check_vma=False,
    )
```

```python
import functools
import math

import jax
import jax.numpy as jnp
from jax import lax
from jax.experimental import pallas as pl
from jax.experimental.pallas import tpu as pltpu
from jax.sharding import PartitionSpec as P

G = 8192
CW = 128
DYSON = 2
LANES = 128


def live_weights(all_energy, batch_live, slots, total_slots, group_ids, frequencies, norm_factor):
    positions = jnp.arange(total_slots, dtype=jnp.int32)
    owner_match = (positions // slots)[:, None] == group_ids[None, :]
    limits = jnp.sum(jnp.where(owner_match, batch_live[None, :], 0), axis=1)
    is_live = (positions % slots < limits).astype(jnp.float32)
    weight = (
        -2.0
        * all_energy[None, :]
        / (all_energy[None, :] * all_energy[None, :] + frequencies[:, None] * frequencies[:, None])
    )
    return weight * is_live[None, :] * norm_factor


def plain_body(pair_density, energies, batch_live, coulomb_root):
    slots = pair_density.shape[0]
    width_own = pair_density.shape[1]
    group_count = lax.axis_size("grp")
    block_count = lax.axis_size("blk")
    total_slots = slots * group_count
    group_index = lax.axis_index("grp")
    block_index = lax.axis_index("blk")
    norm_factor = 1.0 / math.sqrt(total_slots)
    own_root = lax.dynamic_slice_in_dim(coulomb_root, block_index * width_own, width_own)
    group_ids = jnp.arange(group_count, dtype=jnp.int32)
    row_density, all_energy = (
        lax.all_gather(pair_density, "grp", axis=0, tiled=True),
        lax.all_gather(energies.astype(jnp.bfloat16), "grp", axis=0, tiled=True).astype(
            energies.dtype
        ),
    )
    frequencies = 0.6 * jnp.arange(group_count, dtype=jnp.float32)
    weight = live_weights(
        all_energy, batch_live, slots, total_slots, group_ids, frequencies, norm_factor
    )
    scaled = (weight[:, :, None] * row_density.astype(jnp.float32)[None, :, :]).astype(jnp.bfloat16)
    sub_width = width_own // group_count
    my_slice = lax.dynamic_slice_in_dim(row_density, group_index * sub_width, sub_width, 1)
    root_table = jnp.reshape(coulomb_root, (block_count, group_count, sub_width))
    my_roots = jnp.reshape(
        lax.dynamic_index_in_dim(root_table, group_index, 1, keepdims=False), (-1,)
    )
    chi = jnp.einsum(
        "ftc,tk->fck",
        scaled,
        lax.all_gather(my_slice, "blk", axis=1, tiled=True),
        preferred_element_type=jnp.float32,
    )
    quarter = own_root[None, :, None] * chi * my_roots[None, None, :]
    received = lax.all_to_all(
        quarter.astype(jnp.bfloat16), "grp", split_axis=0, concat_axis=0, tiled=True
    )
    received = jnp.reshape(received, (group_count, width_own, block_count, sub_width))
    polarized = jnp.reshape(
        jnp.transpose(received, (1, 2, 0, 3)), (width_own, width_own * block_count)
    )
    lead_blocks = (CW + width_own - 1) // width_own
    lead = quarter[:, :, : lead_blocks * sub_width]
    lead_back = lax.all_to_all(
        lead.astype(jnp.bfloat16), "grp", split_axis=0, concat_axis=0, tiled=True
    ).astype(lead.dtype)
    lead_back = jnp.reshape(lead_back, (group_count, width_own, lead_blocks, sub_width))
    window = jnp.reshape(
        jnp.transpose(lead_back, (1, 2, 0, 3)), (width_own, lead_blocks * width_own)
    )[:, :CW]
    state = window
    for dyson_step in range(DYSON):
        rounded = state.astype(jnp.bfloat16)
        product = jnp.dot(
            polarized,
            lax.all_gather(rounded, "blk", axis=0, tiled=True),
            preferred_element_type=jnp.float32,
        )
        state = window + 8.0 / G * product
    return (polarized[None], state[None])


def pack_rows(batch_live, slots, total, packed):
    ends = jnp.cumsum(batch_live)
    starts = ends - batch_live
    j = jnp.arange(packed, dtype=jnp.int32)
    in_group = (j[:, None] >= starts[None, :]) & (j[:, None] < ends[None, :])
    group_base = jnp.arange(batch_live.shape[0], dtype=jnp.int32) * slots - starts
    source = jnp.sum(jnp.where(in_group, group_base[None, :] + j[:, None], 0), axis=1)
    used = jnp.any(in_group, axis=1)
    source = jnp.where(used, source, -1)
    return source, used


def chi_kernel(n, factor, a_ref, p_ref, w_ref, r_ref, out_ref, s_ref, at_ref, q_ref, u_ref, v_ref):
    i = pl.program_id(0)
    width = a_ref.shape[0]
    split, _, _, sub = p_ref.shape

    def root(k):
        return r_ref[:, k * sub:(k + 1) * sub]

    def spread(k, part):
        part = (part * root(k)).T.astype(jnp.bfloat16)
        return jnp.dot(p_ref[k, 0], part, preferred_element_type=jnp.float32)

    @pl.when(i == 0)
    def _():
        at_ref[:width] = a_ref[...]
        q = (p_ref[0, 0, :, :CW].astype(jnp.float32) * r_ref[:, :CW]).T
        q_ref[...] = q
        at_ref[width:] = (q * w_ref[...]).astype(jnp.bfloat16)
        u_ref[...] = jnp.zeros_like(u_ref)

    @pl.when(i < n)
    def _():
        for k in range(split):
            prod = jnp.dot(at_ref[...], p_ref[k, 0], preferred_element_type=jnp.float32) * root(k)
            out_ref[:, k * sub:(k + 1) * sub] = prod[:width].astype(jnp.bfloat16)
            u_ref[...] += spread(k, prod[width:])

    @pl.when(i == n - 1)
    def _():
        v_ref[...] = (u_ref[...].T * (w_ref[...] * factor)).astype(jnp.bfloat16)

    @pl.when(i >= n)
    def _():
        for k in range(split):
            prod = jnp.dot(v_ref[...], p_ref[k, 0], preferred_element_type=jnp.float32) * root(k)
            u_ref[...] += spread(k, prod)

    @pl.when(i == 2 * n - 1)
    def _():
        x = (q_ref[...] + factor * u_ref[...].T).astype(jnp.bfloat16)
        s_ref[...] = lax.dot_general(
            a_ref[...], x, (((1,), (1,)), ((), ())), preferred_element_type=jnp.float32)


def chi_and_screen(left, pieces, weight, coulomb_root):
    width, packed = left.shape
    split, n, _, sub = pieces.shape
    return pl.pallas_call(
        functools.partial(chi_kernel, n, 8.0 / G),
        grid=(2 * n,),
        out_shape=(
            jax.ShapeDtypeStruct((width, n * split * sub), jnp.bfloat16),
            jax.ShapeDtypeStruct((width, CW), jnp.float32),
        ),
        in_specs=[
            pl.BlockSpec((width, packed), lambda i: (0, 0)),
            pl.BlockSpec((split, 1, packed, sub), lambda i: (0, i % n, 0, 0)),
            pl.BlockSpec((1, packed), lambda i: (0, 0)),
            pl.BlockSpec((1, split * sub), lambda i: (0, i % n)),
        ],
        out_specs=(
            pl.BlockSpec((width, split * sub), lambda i: (0, jnp.minimum(i, n - 1))),
            pl.BlockSpec((width, CW), lambda i: (0, 0)),
        ),
        scratch_shapes=[
            pltpu.VMEM((width + CW, packed), jnp.bfloat16),
            pltpu.VMEM((CW, packed), jnp.float32),
            pltpu.VMEM((packed, CW), jnp.float32),
            pltpu.VMEM((CW, packed), jnp.bfloat16),
        ],
        compiler_params=pltpu.CompilerParams(vmem_limit_bytes=48 * 1024 * 1024),
    )(left, pieces, weight[None, :], coulomb_root[None, :])


def gather_kernel(
    nz, rows_ref, energy_ref, source_ref, out_ref, energies_ref,
    all_ref, pick_ref, own_ref, recv, s_up, s_down, s_y, s_x, s_pair, s_own,
    r_rows, s_rows, s_local, r_energy, s_energy,
):
    g, b = lax.axis_index("grp"), lax.axis_index("blk")
    x, c = g // 2, g % 2
    z, y = b // 2, b % 2
    half = own_ref.shape[1] // 2
    rows = pl.ds(pl.multiple_of(c * half, half), half)
    other_rows = pl.ds(pl.multiple_of((1 - c) * half, half), half)
    to_up, to_down = (g, b + 2), (g, b - 2)
    to_y = (g, z * 2 + 1 - y)
    to_x = ((1 - x) * 2 + c, b)
    to_pair = (x * 2 + 1 - c, b)
    has_up, has_down = z + 1 < nz, z >= 1
    skip_y, own_x = 2 * (1 - x), 2 * x

    def copy(q, bb, sem, to, own=False):
        src = own_ref.at[q, rows] if own else out_ref.at[q, bb, rows]
        return pltpu.make_async_remote_copy(
            src_ref=src, dst_ref=out_ref.at[q, bb, rows], send_sem=sem,
            recv_sem=recv.at[q, bb, c], device_id=to, device_id_type=pl.DeviceIdType.MESH)

    def arrived(q, bb):
        copy(q, bb, s_pair.at[q, bb], to_pair).wait_recv()

    def up(zz, j, own=False):
        return copy(x + j, zz * 2 + y, s_up.at[j, zz], to_up, own)

    def down(zz, j, own=False):
        return copy(x + j, zz * 2 + y, s_down.at[j, zz], to_down, own)

    def over_y(zz, j, own=False):
        return copy(x + j, zz * 2 + y, s_y.at[j, zz], to_y, own)

    def over_x(zz, yy, j):
        return copy(x + j, zz * 2 + yy, s_x.at[j, zz * 2 + yy], to_x)

    def over_pair(q, bb):
        return copy(q, bb, s_pair.at[q, bb], to_pair)

    def takes_y(zz, j):
        return (zz % 4 != 1) | (j != skip_y)

    def other_y_takes_x(zz, j):
        return ((zz % 4 != 1) & (j == own_x)) | ((zz % 4 == 1) & (j != skip_y))

    def when(condition, make, act):
        @pl.when(condition)
        def _():
            getattr(make(), act)()

    def from_z(zz, j, below, valid):
        @pl.when(valid)
        def _():
            q, bb = x + j, zz * 2 + y
            arrived(q, bb)
            if below:
                when(has_up, lambda: up(zz, j), "start")
            else:
                when(has_down, lambda: down(zz, j), "start")
            when(takes_y(zz, j), lambda: over_y(zz, j), "start")
            when(j == own_x, lambda: over_x(zz, y, j), "start")
            over_pair(q, bb).start()

    def from_y(zz, j, valid):
        @pl.when(valid & takes_y(zz, j))
        def _():
            q, bb = x + j, zz * 2 + 1 - y
            arrived(q, bb)
            when(other_y_takes_x(zz, j), lambda: over_x(zz, 1 - y, j), "start")
            over_pair(q, bb).start()

    def from_x(zz, same_y, valid):
        bb = zz * 2 + (y if same_y else 1 - y)

        def take(q):
            arrived(q, bb)
            over_pair(q, bb).start()

        if same_y:
            @pl.when(valid)
            def _():
                take(3 * (1 - x))
        else:
            @pl.when(valid & (zz % 4 != 1))
            def _():
                take(3 * (1 - x))

            @pl.when(valid & (zz % 4 == 1))
            def _():
                take(2 * (1 - x))
                take(2 * (1 - x) + 1)

    def at_distance(d):
        if d == 0:
            return [(z, True, z >= 0)]
        return [(z - d, True, z >= d), (z + d, False, z + d < nz)]

    barrier = pltpu.get_barrier_semaphore()

    def greet(to):
        pl.semaphore_signal(barrier, inc=1, device_id=to, device_id_type=pl.DeviceIdType.MESH)

    for to in (to_y, to_x, to_pair):
        greet(to)
    pl.when(has_up)(lambda: greet(to_up))
    pl.when(has_down)(lambda: greet(to_down))
    peers = 3 + has_up.astype(jnp.int32) + has_down.astype(jnp.int32)
    pl.semaphore_wait(barrier, peers)

    slots, packed, sub = rows_ref.shape[0], own_ref.shape[1], own_ref.shape[2]
    g_x, g_pair = (1 - x) * 2 + c, x * 2 + 1 - c
    g_far = (1 - x) * 2 + 1 - c

    def span(k):
        return pl.ds(pl.multiple_of(k * slots, slots), slots)

    def order(j):
        return jnp.where(j < 3, x + j, 3 * (1 - x))

    def rows_to(q, way, to, who):
        dst = all_ref.at[q, span(who)]
        columns = pl.ds(pl.multiple_of(q * sub, sub), sub)
        return pltpu.make_async_remote_copy(
            src_ref=dst if way == 2 else rows_ref.at[:, columns], dst_ref=dst,
            send_sem=s_rows.at[way, q], recv_sem=r_rows.at[q, who], device_id=to,
            device_id_type=pl.DeviceIdType.MESH)

    def rows_local(q):
        columns = pl.ds(pl.multiple_of(q * sub, sub), sub)
        return pltpu.make_async_copy(rows_ref.at[:, columns], all_ref.at[q, span(g)], s_local.at[q])

    def energy_to(way, to, who):
        return pltpu.make_async_remote_copy(
            src_ref=energies_ref.at[who] if way == 2 else energy_ref.at[0],
            dst_ref=energies_ref.at[who], send_sem=s_energy.at[way], recv_sem=r_energy.at[who],
            device_id=to, device_id_type=pl.DeviceIdType.MESH)

    for j in range(4):
        q = order(j)
        rows_to(q, 0, to_x, g).start()
        rows_to(q, 1, to_pair, g).start()
        rows_local(q).start()
    energy_to(0, to_x, g).start()
    energy_to(1, to_pair, g).start()
    keep_energy = pltpu.make_async_copy(energy_ref.at[0], energies_ref.at[g], s_local.at[4])
    keep_energy.start()

    @pl.loop(0, packed // 128)
    def _(k):
        part = pl.ds(pl.multiple_of(k * 128, 128), 128)
        at = lax.broadcasted_iota(jnp.int32, (128, pick_ref.shape[1]), 1)
        pick_ref[part] = (source_ref[part] == at).astype(jnp.float32).astype(jnp.bfloat16)

    def keep(q):
        return pltpu.make_async_copy(own_ref.at[q], out_ref.at[q, b], s_own.at[q])

    @pl.loop(0, 4)
    def _(j):
        q = order(j)
        rows_to(q, 0, to_x, g_x).wait_recv()
        rows_to(q, 2, to_pair, g_x).start()
        rows_local(q).wait()
        rows_to(q, 1, to_pair, g_pair).wait_recv()
        rows_to(q, 2, to_pair, g_far).wait_recv()
        own_ref[q] = jnp.dot(
            pick_ref[...], all_ref[q], preferred_element_type=jnp.float32).astype(jnp.bfloat16)
        carried = j < 3
        when(carried & has_up, lambda: up(z, j, True), "start")
        when(carried & has_down, lambda: down(z, j, True), "start")
        when(carried & takes_y(z, j), lambda: over_y(z, j, True), "start")
        keep(q).start()

    energy_to(0, to_x, g_x).wait_recv()
    energy_to(2, to_pair, g_x).start()

    for s in range(nz + 1):
        for j in range(3):
            if 1 <= s + 1 < nz:
                for zz, below, valid in at_distance(s + 1):
                    from_z(zz, j, below, valid)
            if s < nz:
                for zz, _, valid in at_distance(s):
                    from_y(zz, j, valid)
        if 1 <= s < nz:
            for zz, _, valid in at_distance(s):
                from_x(zz, True, valid)
        if s >= 1:
            for zz, _, valid in at_distance(s - 1):
                from_x(zz, False, valid)

    def from_pair(q, bb):
        pltpu.make_async_remote_copy(
            src_ref=out_ref.at[q, bb, other_rows], dst_ref=out_ref.at[q, bb, other_rows],
            send_sem=s_pair.at[q, bb], recv_sem=recv.at[q, bb, 1 - c],
            device_id=to_pair, device_id_type=pl.DeviceIdType.MESH).wait_recv()
        over_pair(q, bb).wait_send()

    energy_to(1, to_pair, g_pair).wait_recv()
    energy_to(2, to_pair, g_far).wait_recv()
    energy_to(0, to_x, g).wait_send()
    energy_to(1, to_pair, g).wait_send()
    energy_to(2, to_pair, g_x).wait_send()
    keep_energy.wait()
    for j in range(4):
        q = order(j)
        rows_to(q, 0, to_x, g).wait_send()
        rows_to(q, 1, to_pair, g).wait_send()
        rows_to(q, 2, to_pair, g_x).wait_send()
        keep(q).wait()
    for j in range(3):
        when(has_up, lambda: up(z, j, True), "wait_send")
        when(has_down, lambda: down(z, j, True), "wait_send")
        when(takes_y(z, j), lambda: over_y(z, j, True), "wait_send")
    for d in range(nz):
        for zz, below, valid in at_distance(d):
            for j in range(3):
                if d >= 1:
                    if below:
                        when(valid & has_up, lambda: up(zz, j), "wait_send")
                    else:
                        when(valid & has_down, lambda: down(zz, j), "wait_send")
                    when(valid & takes_y(zz, j), lambda: over_y(zz, j), "wait_send")
                    when(valid & (j == own_x), lambda: over_x(zz, y, j), "wait_send")
                when(valid & other_y_takes_x(zz, j), lambda: over_x(zz, 1 - y, j), "wait_send")
            for same_y in (True, False):
                if d >= 1 or not same_y:
                    for q in range(4):
                        pl.when(valid)(
                            lambda q=q: from_pair(q, zz * 2 + (y if same_y else 1 - y)))


def gather_pieces(pair_density, energies, source, blocks, split):
    slots, width = pair_density.shape
    packed = source.shape[0]
    sub, nz = width // split, blocks // 2
    dma = pltpu.SemaphoreType.DMA
    vmem = pl.BlockSpec(memory_space=pltpu.VMEM)
    return pl.pallas_call(
        functools.partial(gather_kernel, nz),
        out_shape=(
            jax.ShapeDtypeStruct((split, blocks, packed, sub), jnp.bfloat16),
            jax.ShapeDtypeStruct((split, 1, slots), jnp.float32),
        ),
        in_specs=[vmem, vmem, vmem],
        out_specs=(pl.BlockSpec(memory_space=pl.ANY), vmem),
        scratch_shapes=[
            pltpu.VMEM((split, split * slots, sub), jnp.bfloat16),
            pltpu.VMEM((packed, split * slots), jnp.bfloat16),
            pltpu.VMEM((split, packed, sub), jnp.bfloat16),
            dma((split, blocks, 2)), dma((3, nz)), dma((3, nz)), dma((3, nz)),
            dma((3, blocks)), dma((split, blocks)), dma((split,)),
            dma((split, split)), dma((3, split)), dma((split + 1,)), dma((split,)), dma((3,)),
        ],
        compiler_params=pltpu.CompilerParams(
            collective_id=0, has_side_effects=True, vmem_limit_bytes=40 * 1024 * 1024),
    )(pair_density, energies[None, None, :], source[:, None])


def body(pair_density, energies, batch_live, coulomb_root):
    slots, width = pair_density.shape
    group_count = lax.axis_size("grp")
    blocks = lax.axis_size("blk")
    total = slots * group_count
    packed = total * 5 // 8
    group_index = lax.axis_index("grp")
    block_index = lax.axis_index("blk")
    own_root = lax.dynamic_slice_in_dim(coulomb_root, block_index * width, width)

    source, used = pack_rows(batch_live, slots, total, packed)
    pieces, all_energy = gather_pieces(pair_density, energies, source, blocks, group_count)
    pick = source[:, None] == jnp.arange(total, dtype=jnp.int32)[None, :]
    energy = jnp.sum(jnp.where(pick, jnp.reshape(all_energy, (1, total)), 0.0), axis=1)
    energy = jnp.where(used, energy, 1.0)
    frequency = 0.6 * group_index.astype(jnp.float32)
    weight = -2.0 * energy / (energy * energy + frequency * frequency)
    weight = jnp.where(used, weight, 0.0) * (1.0 / math.sqrt(total))
    own = lax.dynamic_index_in_dim(pieces, block_index, 1, keepdims=False)
    own = jnp.reshape(jnp.swapaxes(own, 1, 2), (width, packed)).astype(jnp.float32)
    left = (own * weight[None, :] * own_root[:, None]).astype(jnp.bfloat16)
    polarized, screened = chi_and_screen(left, pieces, weight, coulomb_root)
    return (polarized[None], screened[None])


def solution(mesh):
    placed = (P("grp", "blk"), P("grp"), P(), P())
    aligned = (
        mesh.shape["grp"] == 4
        and mesh.shape["blk"] % 2 == 0
        and (G // mesh.shape["blk"]) % (LANES * mesh.shape["grp"]) == 0
    )
    return jax.shard_map(
        body if aligned else plain_body,
        mesh=mesh,
        in_specs=placed,
        out_specs=(P("grp", "blk", None), P("grp", "blk", None)),
        check_vma=False,
    )
```

```python
import functools
import math

import jax
import jax.numpy as jnp
from jax import lax
from jax.experimental import pallas as pl
from jax.experimental.pallas import tpu as pltpu
from jax.sharding import PartitionSpec as P

G = 8192
CW = 128
DYSON = 2
LANES = 128


def live_weights(all_energy, batch_live, slots, total_slots, group_ids, frequencies, norm_factor):
    positions = jnp.arange(total_slots, dtype=jnp.int32)
    owner_match = (positions // slots)[:, None] == group_ids[None, :]
    limits = jnp.sum(jnp.where(owner_match, batch_live[None, :], 0), axis=1)
    is_live = (positions % slots < limits).astype(jnp.float32)
    weight = (
        -2.0
        * all_energy[None, :]
        / (all_energy[None, :] * all_energy[None, :] + frequencies[:, None] * frequencies[:, None])
    )
    return weight * is_live[None, :] * norm_factor


def plain_body(pair_density, energies, batch_live, coulomb_root):
    slots = pair_density.shape[0]
    width_own = pair_density.shape[1]
    group_count = lax.axis_size("grp")
    block_count = lax.axis_size("blk")
    total_slots = slots * group_count
    group_index = lax.axis_index("grp")
    block_index = lax.axis_index("blk")
    norm_factor = 1.0 / math.sqrt(total_slots)
    own_root = lax.dynamic_slice_in_dim(coulomb_root, block_index * width_own, width_own)
    group_ids = jnp.arange(group_count, dtype=jnp.int32)
    row_density, all_energy = (
        lax.all_gather(pair_density, "grp", axis=0, tiled=True),
        lax.all_gather(energies.astype(jnp.bfloat16), "grp", axis=0, tiled=True).astype(
            energies.dtype
        ),
    )
    frequencies = 0.6 * jnp.arange(group_count, dtype=jnp.float32)
    weight = live_weights(
        all_energy, batch_live, slots, total_slots, group_ids, frequencies, norm_factor
    )
    scaled = (weight[:, :, None] * row_density.astype(jnp.float32)[None, :, :]).astype(jnp.bfloat16)
    sub_width = width_own // group_count
    my_slice = lax.dynamic_slice_in_dim(row_density, group_index * sub_width, sub_width, 1)
    root_table = jnp.reshape(coulomb_root, (block_count, group_count, sub_width))
    my_roots = jnp.reshape(
        lax.dynamic_index_in_dim(root_table, group_index, 1, keepdims=False), (-1,)
    )
    chi = jnp.einsum(
        "ftc,tk->fck",
        scaled,
        lax.all_gather(my_slice, "blk", axis=1, tiled=True),
        preferred_element_type=jnp.float32,
    )
    quarter = own_root[None, :, None] * chi * my_roots[None, None, :]
    received = lax.all_to_all(
        quarter.astype(jnp.bfloat16), "grp", split_axis=0, concat_axis=0, tiled=True
    )
    received = jnp.reshape(received, (group_count, width_own, block_count, sub_width))
    polarized = jnp.reshape(
        jnp.transpose(received, (1, 2, 0, 3)), (width_own, width_own * block_count)
    )
    lead_blocks = (CW + width_own - 1) // width_own
    lead = quarter[:, :, : lead_blocks * sub_width]
    lead_back = lax.all_to_all(
        lead.astype(jnp.bfloat16), "grp", split_axis=0, concat_axis=0, tiled=True
    ).astype(lead.dtype)
    lead_back = jnp.reshape(lead_back, (group_count, width_own, lead_blocks, sub_width))
    window = jnp.reshape(
        jnp.transpose(lead_back, (1, 2, 0, 3)), (width_own, lead_blocks * width_own)
    )[:, :CW]
    state = window
    for dyson_step in range(DYSON):
        rounded = state.astype(jnp.bfloat16)
        product = jnp.dot(
            polarized,
            lax.all_gather(rounded, "blk", axis=0, tiled=True),
            preferred_element_type=jnp.float32,
        )
        state = window + 8.0 / G * product
    return (polarized[None], state[None])


def pack_rows(batch_live, slots, total, packed):
    ends = jnp.cumsum(batch_live)
    starts = ends - batch_live
    j = jnp.arange(packed, dtype=jnp.int32)
    in_group = (j[:, None] >= starts[None, :]) & (j[:, None] < ends[None, :])
    group_base = jnp.arange(batch_live.shape[0], dtype=jnp.int32) * slots - starts
    source = jnp.sum(jnp.where(in_group, group_base[None, :] + j[:, None], 0), axis=1)
    used = jnp.any(in_group, axis=1)
    source = jnp.where(used, source, -1)
    return source, used


def chi_kernel(
    n, factor, own_ref, p_ref, w_ref, own_root_ref, r_ref, out_ref, s_ref,
    at_ref, q_ref, u_ref, v_ref, t_ref,
):
    i = pl.program_id(0)
    width = at_ref.shape[0] - CW
    split, _, _, sub = p_ref.shape

    def root(k):
        return r_ref[:, k * sub:(k + 1) * sub]

    def spread(k, part):
        part = (part * root(k)).T.astype(jnp.bfloat16)
        return jnp.dot(p_ref[k, 0], part, preferred_element_type=jnp.float32)

    @pl.when(i == 0)
    def _():
        for k in range(split):
            part = slice(k * sub, (k + 1) * sub)
            left = (own_ref[k].astype(jnp.float32) * own_root_ref[:, part]).T
            at_ref[part] = (left * w_ref[...]).astype(jnp.bfloat16)
        q = (p_ref[0, 0, :, :CW].astype(jnp.float32) * r_ref[:, :CW]).T
        q_ref[...] = q
        at_ref[width:] = (q * w_ref[...]).astype(jnp.bfloat16)
        u_ref[...] = jnp.zeros_like(u_ref)

    @pl.when(i < n)
    def _():
        for k in range(split):
            prod = jnp.dot(at_ref[...], p_ref[k, 0], preferred_element_type=jnp.float32) * root(k)
            out_ref[:, k * sub:(k + 1) * sub] = prod[:width].astype(jnp.bfloat16)
            t_ref[:, k * sub:(k + 1) * sub] = prod[width:]

    @pl.when(i < n)
    def _():
        for k in range(split):
            u_ref[...] += spread(k, t_ref[:, k * sub:(k + 1) * sub])

    @pl.when(i == n - 1)
    def _():
        v_ref[...] = (u_ref[...].T * (w_ref[...] * factor)).astype(jnp.bfloat16)

    @pl.when(i >= n)
    def _():
        for k in range(split):
            prod = jnp.dot(v_ref[...], p_ref[k, 0], preferred_element_type=jnp.float32) * root(k)
            u_ref[...] += spread(k, prod)

    @pl.when(i == 2 * n - 1)
    def _():
        x = (q_ref[...] + factor * u_ref[...].T).astype(jnp.bfloat16)
        s_ref[...] = lax.dot_general(
            at_ref[:width], x, (((1,), (1,)), ((), ())), preferred_element_type=jnp.float32)


def chi_and_screen(own, pieces, weight, own_root, coulomb_root):
    split, n, packed, sub = pieces.shape
    width = split * sub
    return pl.pallas_call(
        functools.partial(chi_kernel, n, 8.0 / G),
        grid=(2 * n,),
        out_shape=(
            jax.ShapeDtypeStruct((width, n * split * sub), jnp.bfloat16),
            jax.ShapeDtypeStruct((width, CW), jnp.float32),
        ),
        in_specs=[
            pl.BlockSpec((split, packed, sub), lambda i: (0, 0, 0)),
            pl.BlockSpec((split, 1, packed, sub), lambda i: (0, i % n, 0, 0)),
            pl.BlockSpec((1, packed), lambda i: (0, 0)),
            pl.BlockSpec((1, width), lambda i: (0, 0)),
            pl.BlockSpec((1, split * sub), lambda i: (0, i % n)),
        ],
        out_specs=(
            pl.BlockSpec((width, split * sub), lambda i: (0, jnp.minimum(i, n - 1))),
            pl.BlockSpec((width, CW), lambda i: (0, 0)),
        ),
        scratch_shapes=[
            pltpu.VMEM((width + CW, packed), jnp.bfloat16),
            pltpu.VMEM((CW, packed), jnp.float32),
            pltpu.VMEM((packed, CW), jnp.float32),
            pltpu.VMEM((CW, packed), jnp.bfloat16),
            pltpu.VMEM((CW, width), jnp.float32),
        ],
        compiler_params=pltpu.CompilerParams(vmem_limit_bytes=48 * 1024 * 1024),
    )(own, pieces, weight[None, :], own_root[None, :], coulomb_root[None, :])


def gather_kernel(
    nz, rows_ref, energy_ref, source_ref, out_ref, energies_ref, own_ref,
    all_ref, pick_ref, recv, s_up, s_down, s_y, s_x, s_pair, s_own,
    r_rows, s_rows, s_local, r_energy, s_energy,
):
    g, b = lax.axis_index("grp"), lax.axis_index("blk")
    x, c = g // 2, g % 2
    z, y = b // 2, b % 2
    half = own_ref.shape[1] // 2
    rows = pl.ds(pl.multiple_of(c * half, half), half)
    other_rows = pl.ds(pl.multiple_of((1 - c) * half, half), half)
    to_up, to_down = (g, b + 2), (g, b - 2)
    to_y = (g, z * 2 + 1 - y)
    to_x = ((1 - x) * 2 + c, b)
    to_pair = (x * 2 + 1 - c, b)
    has_up, has_down = z + 1 < nz, z >= 1
    skip_y, own_x = 2 * (1 - x), 2 * x

    def copy(q, bb, sem, to, own=False):
        src = own_ref.at[q, rows] if own else out_ref.at[q, bb, rows]
        return pltpu.make_async_remote_copy(
            src_ref=src, dst_ref=out_ref.at[q, bb, rows], send_sem=sem,
            recv_sem=recv.at[q, bb, c], device_id=to, device_id_type=pl.DeviceIdType.MESH)

    def arrived(q, bb):
        copy(q, bb, s_pair.at[q, bb], to_pair).wait_recv()

    def up(zz, j, own=False):
        return copy(x + j, zz * 2 + y, s_up.at[j, zz], to_up, own)

    def down(zz, j, own=False):
        return copy(x + j, zz * 2 + y, s_down.at[j, zz], to_down, own)

    def over_y(zz, j, own=False):
        return copy(x + j, zz * 2 + y, s_y.at[j, zz], to_y, own)

    def over_x(zz, yy, j):
        return copy(x + j, zz * 2 + yy, s_x.at[j, zz * 2 + yy], to_x)

    def over_pair(q, bb):
        return copy(q, bb, s_pair.at[q, bb], to_pair)

    def takes_y(zz, j):
        return (zz % 4 != 1) | (j != skip_y)

    def other_y_takes_x(zz, j):
        return ((zz % 4 != 1) & (j == own_x)) | ((zz % 4 == 1) & (j != skip_y))

    def when(condition, make, act):
        @pl.when(condition)
        def _():
            getattr(make(), act)()

    def from_z(zz, j, below, valid):
        @pl.when(valid)
        def _():
            q, bb = x + j, zz * 2 + y
            arrived(q, bb)
            if below:
                when(has_up, lambda: up(zz, j), "start")
            else:
                when(has_down, lambda: down(zz, j), "start")
            when(takes_y(zz, j), lambda: over_y(zz, j), "start")
            when(j == own_x, lambda: over_x(zz, y, j), "start")
            over_pair(q, bb).start()

    def from_y(zz, j, valid):
        @pl.when(valid & takes_y(zz, j))
        def _():
            q, bb = x + j, zz * 2 + 1 - y
            arrived(q, bb)
            when(other_y_takes_x(zz, j), lambda: over_x(zz, 1 - y, j), "start")
            over_pair(q, bb).start()

    def from_x(zz, same_y, valid):
        bb = zz * 2 + (y if same_y else 1 - y)

        def take(q):
            arrived(q, bb)
            over_pair(q, bb).start()

        if same_y:
            @pl.when(valid)
            def _():
                take(3 * (1 - x))
        else:
            @pl.when(valid & (zz % 4 != 1))
            def _():
                take(3 * (1 - x))

            @pl.when(valid & (zz % 4 == 1))
            def _():
                take(2 * (1 - x))
                take(2 * (1 - x) + 1)

    def at_distance(d):
        if d == 0:
            return [(z, True, z >= 0)]
        return [(z - d, True, z >= d), (z + d, False, z + d < nz)]

    barrier = pltpu.get_barrier_semaphore()

    def greet(to):
        pl.semaphore_signal(barrier, inc=1, device_id=to, device_id_type=pl.DeviceIdType.MESH)

    for to in (to_y, to_x, to_pair):
        greet(to)
    pl.when(has_up)(lambda: greet(to_up))
    pl.when(has_down)(lambda: greet(to_down))
    peers = 3 + has_up.astype(jnp.int32) + has_down.astype(jnp.int32)
    pl.semaphore_wait(barrier, peers)

    slots, packed, sub = rows_ref.shape[0], own_ref.shape[1], own_ref.shape[2]
    g_x, g_pair = (1 - x) * 2 + c, x * 2 + 1 - c
    g_far = (1 - x) * 2 + 1 - c

    def span(k):
        return pl.ds(pl.multiple_of(k * slots, slots), slots)

    def order(j):
        return jnp.where(j < 3, x + j, 3 * (1 - x))

    def rows_to(q, way, to, who):
        dst = all_ref.at[q, span(who)]
        columns = pl.ds(pl.multiple_of(q * sub, sub), sub)
        return pltpu.make_async_remote_copy(
            src_ref=dst if way == 2 else rows_ref.at[:, columns], dst_ref=dst,
            send_sem=s_rows.at[way, q], recv_sem=r_rows.at[q, who], device_id=to,
            device_id_type=pl.DeviceIdType.MESH)

    def rows_local(q):
        columns = pl.ds(pl.multiple_of(q * sub, sub), sub)
        return pltpu.make_async_copy(rows_ref.at[:, columns], all_ref.at[q, span(g)], s_local.at[q])

    def energy_to(way, to, who):
        return pltpu.make_async_remote_copy(
            src_ref=energies_ref.at[who] if way == 2 else energy_ref.at[0],
            dst_ref=energies_ref.at[who], send_sem=s_energy.at[way], recv_sem=r_energy.at[who],
            device_id=to, device_id_type=pl.DeviceIdType.MESH)

    for j in range(4):
        q = order(j)
        rows_to(q, 0, to_x, g).start()
        rows_to(q, 1, to_pair, g).start()
        rows_local(q).start()
    energy_to(0, to_x, g).start()
    energy_to(1, to_pair, g).start()
    keep_energy = pltpu.make_async_copy(energy_ref.at[0], energies_ref.at[g], s_local.at[4])
    keep_energy.start()

    @pl.loop(0, packed // 128)
    def _(k):
        part = pl.ds(pl.multiple_of(k * 128, 128), 128)
        at = lax.broadcasted_iota(jnp.int32, (128, pick_ref.shape[1]), 1)
        pick_ref[part] = (source_ref[part] == at).astype(jnp.float32).astype(jnp.bfloat16)

    def keep(q):
        return pltpu.make_async_copy(own_ref.at[q], out_ref.at[q, b], s_own.at[q])

    @pl.loop(0, 4)
    def _(j):
        q = order(j)
        rows_to(q, 0, to_x, g_x).wait_recv()
        rows_to(q, 2, to_pair, g_x).start()
        rows_local(q).wait()
        rows_to(q, 1, to_pair, g_pair).wait_recv()
        rows_to(q, 2, to_pair, g_far).wait_recv()
        own_ref[q] = jnp.dot(
            pick_ref[...], all_ref[q], preferred_element_type=jnp.float32).astype(jnp.bfloat16)
        carried = j < 3
        when(carried & has_up, lambda: up(z, j, True), "start")
        when(carried & has_down, lambda: down(z, j, True), "start")
        when(carried & takes_y(z, j), lambda: over_y(z, j, True), "start")
        keep(q).start()

    energy_to(0, to_x, g_x).wait_recv()
    energy_to(2, to_pair, g_x).start()

    for s in range(nz + 1):
        for j in range(3):
            if 1 <= s + 1 < nz:
                for zz, below, valid in at_distance(s + 1):
                    from_z(zz, j, below, valid)
            if s < nz:
                for zz, _, valid in at_distance(s):
                    from_y(zz, j, valid)
        if 1 <= s < nz:
            for zz, _, valid in at_distance(s):
                from_x(zz, True, valid)
        if s >= 1:
            for zz, _, valid in at_distance(s - 1):
                from_x(zz, False, valid)

    def from_pair(q, bb):
        pltpu.make_async_remote_copy(
            src_ref=out_ref.at[q, bb, other_rows], dst_ref=out_ref.at[q, bb, other_rows],
            send_sem=s_pair.at[q, bb], recv_sem=recv.at[q, bb, 1 - c],
            device_id=to_pair, device_id_type=pl.DeviceIdType.MESH).wait_recv()
        over_pair(q, bb).wait_send()

    energy_to(1, to_pair, g_pair).wait_recv()
    energy_to(2, to_pair, g_far).wait_recv()
    energy_to(0, to_x, g).wait_send()
    energy_to(1, to_pair, g).wait_send()
    energy_to(2, to_pair, g_x).wait_send()
    keep_energy.wait()
    for j in range(4):
        q = order(j)
        rows_to(q, 0, to_x, g).wait_send()
        rows_to(q, 1, to_pair, g).wait_send()
        rows_to(q, 2, to_pair, g_x).wait_send()
        keep(q).wait()
    for j in range(3):
        when(has_up, lambda: up(z, j, True), "wait_send")
        when(has_down, lambda: down(z, j, True), "wait_send")
        when(takes_y(z, j), lambda: over_y(z, j, True), "wait_send")
    for d in range(nz):
        for zz, below, valid in at_distance(d):
            for j in range(3):
                if d >= 1:
                    if below:
                        when(valid & has_up, lambda: up(zz, j), "wait_send")
                    else:
                        when(valid & has_down, lambda: down(zz, j), "wait_send")
                    when(valid & takes_y(zz, j), lambda: over_y(zz, j), "wait_send")
                    when(valid & (j == own_x), lambda: over_x(zz, y, j), "wait_send")
                when(valid & other_y_takes_x(zz, j), lambda: over_x(zz, 1 - y, j), "wait_send")
            for same_y in (True, False):
                if d >= 1 or not same_y:
                    for q in range(4):
                        pl.when(valid)(
                            lambda q=q: from_pair(q, zz * 2 + (y if same_y else 1 - y)))


def gather_pieces(pair_density, energies, source, blocks, split):
    slots, width = pair_density.shape
    packed = source.shape[0]
    sub, nz = width // split, blocks // 2
    dma = pltpu.SemaphoreType.DMA
    vmem = pl.BlockSpec(memory_space=pltpu.VMEM)
    return pl.pallas_call(
        functools.partial(gather_kernel, nz),
        out_shape=(
            jax.ShapeDtypeStruct((split, blocks, packed, sub), jnp.bfloat16),
            jax.ShapeDtypeStruct((split, 1, slots), jnp.float32),
            jax.ShapeDtypeStruct((split, packed, sub), jnp.bfloat16),
        ),
        in_specs=[vmem, vmem, vmem],
        out_specs=(pl.BlockSpec(memory_space=pl.ANY), vmem, vmem),
        scratch_shapes=[
            pltpu.VMEM((split, split * slots, sub), jnp.bfloat16),
            pltpu.VMEM((packed, split * slots), jnp.bfloat16),
            dma((split, blocks, 2)), dma((3, nz)), dma((3, nz)), dma((3, nz)),
            dma((3, blocks)), dma((split, blocks)), dma((split,)),
            dma((split, split)), dma((3, split)), dma((split + 1,)), dma((split,)), dma((3,)),
        ],
        compiler_params=pltpu.CompilerParams(
            collective_id=0, has_side_effects=True, vmem_limit_bytes=40 * 1024 * 1024),
    )(pair_density, energies[None, None, :], source[:, None])


def body(pair_density, energies, batch_live, coulomb_root):
    slots, width = pair_density.shape
    group_count = lax.axis_size("grp")
    blocks = lax.axis_size("blk")
    total = slots * group_count
    packed = total * 5 // 8
    group_index = lax.axis_index("grp")
    block_index = lax.axis_index("blk")
    own_root = lax.dynamic_slice_in_dim(coulomb_root, block_index * width, width)

    source, used = pack_rows(batch_live, slots, total, packed)
    pieces, all_energy, own = gather_pieces(pair_density, energies, source, blocks, group_count)
    pick = source[:, None] == jnp.arange(total, dtype=jnp.int32)[None, :]
    energy = jnp.sum(jnp.where(pick, jnp.reshape(all_energy, (1, total)), 0.0), axis=1)
    energy = jnp.where(used, energy, 1.0)
    frequency = 0.6 * group_index.astype(jnp.float32)
    weight = -2.0 * energy / (energy * energy + frequency * frequency)
    weight = jnp.where(used, weight, 0.0) * (1.0 / math.sqrt(total))
    polarized, screened = chi_and_screen(own, pieces, weight, own_root, coulomb_root)
    return (polarized[None], screened[None])


def solution(mesh):
    placed = (P("grp", "blk"), P("grp"), P(), P())
    aligned = (
        mesh.shape["grp"] == 4
        and mesh.shape["blk"] % 2 == 0
        and (G // mesh.shape["blk"]) % (LANES * mesh.shape["grp"]) == 0
    )
    return jax.shard_map(
        body if aligned else plain_body,
        mesh=mesh,
        in_specs=placed,
        out_specs=(P("grp", "blk", None), P("grp", "blk", None)),
        check_vma=False,
    )
```

```python
import functools
import math

import jax
import jax.numpy as jnp
from jax import lax
from jax.experimental import pallas as pl
from jax.experimental.pallas import tpu as pltpu
from jax.sharding import PartitionSpec as P

G = 8192
CW = 128
DYSON = 2
LANES = 128


def live_weights(all_energy, batch_live, slots, total_slots, group_ids, frequencies, norm_factor):
    positions = jnp.arange(total_slots, dtype=jnp.int32)
    owner_match = (positions // slots)[:, None] == group_ids[None, :]
    limits = jnp.sum(jnp.where(owner_match, batch_live[None, :], 0), axis=1)
    is_live = (positions % slots < limits).astype(jnp.float32)
    weight = (
        -2.0
        * all_energy[None, :]
        / (all_energy[None, :] * all_energy[None, :] + frequencies[:, None] * frequencies[:, None])
    )
    return weight * is_live[None, :] * norm_factor


def plain_body(pair_density, energies, batch_live, coulomb_root):
    slots = pair_density.shape[0]
    width_own = pair_density.shape[1]
    group_count = lax.axis_size("grp")
    block_count = lax.axis_size("blk")
    total_slots = slots * group_count
    group_index = lax.axis_index("grp")
    block_index = lax.axis_index("blk")
    norm_factor = 1.0 / math.sqrt(total_slots)
    own_root = lax.dynamic_slice_in_dim(coulomb_root, block_index * width_own, width_own)
    group_ids = jnp.arange(group_count, dtype=jnp.int32)
    row_density, all_energy = (
        lax.all_gather(pair_density, "grp", axis=0, tiled=True),
        lax.all_gather(energies.astype(jnp.bfloat16), "grp", axis=0, tiled=True).astype(
            energies.dtype
        ),
    )
    frequencies = 0.6 * jnp.arange(group_count, dtype=jnp.float32)
    weight = live_weights(
        all_energy, batch_live, slots, total_slots, group_ids, frequencies, norm_factor
    )
    scaled = (weight[:, :, None] * row_density.astype(jnp.float32)[None, :, :]).astype(jnp.bfloat16)
    sub_width = width_own // group_count
    my_slice = lax.dynamic_slice_in_dim(row_density, group_index * sub_width, sub_width, 1)
    root_table = jnp.reshape(coulomb_root, (block_count, group_count, sub_width))
    my_roots = jnp.reshape(
        lax.dynamic_index_in_dim(root_table, group_index, 1, keepdims=False), (-1,)
    )
    chi = jnp.einsum(
        "ftc,tk->fck",
        scaled,
        lax.all_gather(my_slice, "blk", axis=1, tiled=True),
        preferred_element_type=jnp.float32,
    )
    quarter = own_root[None, :, None] * chi * my_roots[None, None, :]
    received = lax.all_to_all(
        quarter.astype(jnp.bfloat16), "grp", split_axis=0, concat_axis=0, tiled=True
    )
    received = jnp.reshape(received, (group_count, width_own, block_count, sub_width))
    polarized = jnp.reshape(
        jnp.transpose(received, (1, 2, 0, 3)), (width_own, width_own * block_count)
    )
    lead_blocks = (CW + width_own - 1) // width_own
    lead = quarter[:, :, : lead_blocks * sub_width]
    lead_back = lax.all_to_all(
        lead.astype(jnp.bfloat16), "grp", split_axis=0, concat_axis=0, tiled=True
    ).astype(lead.dtype)
    lead_back = jnp.reshape(lead_back, (group_count, width_own, lead_blocks, sub_width))
    window = jnp.reshape(
        jnp.transpose(lead_back, (1, 2, 0, 3)), (width_own, lead_blocks * width_own)
    )[:, :CW]
    state = window
    for dyson_step in range(DYSON):
        rounded = state.astype(jnp.bfloat16)
        product = jnp.dot(
            polarized,
            lax.all_gather(rounded, "blk", axis=0, tiled=True),
            preferred_element_type=jnp.float32,
        )
        state = window + 8.0 / G * product
    return (polarized[None], state[None])


def pack_rows(batch_live, slots, total, packed):
    ends = jnp.cumsum(batch_live)
    starts = ends - batch_live
    j = jnp.arange(packed, dtype=jnp.int32)
    in_group = (j[:, None] >= starts[None, :]) & (j[:, None] < ends[None, :])
    group_base = jnp.arange(batch_live.shape[0], dtype=jnp.int32) * slots - starts
    source = jnp.sum(jnp.where(in_group, group_base[None, :] + j[:, None], 0), axis=1)
    used = jnp.any(in_group, axis=1)
    source = jnp.where(used, source, -1)
    return source, used


def chi_kernel(
    n, factor, own_ref, p_ref, w_ref, own_root_ref, r_ref, out_ref, s_ref,
    at_ref, q_ref, u_ref, v_ref, t_ref,
):
    i = pl.program_id(0)
    width = at_ref.shape[0] - CW
    split, _, _, sub = p_ref.shape

    def root(k):
        return r_ref[:, k * sub:(k + 1) * sub]

    def spread(k, part):
        part = (part * root(k)).T.astype(jnp.bfloat16)
        return jnp.dot(p_ref[k, 0], part, preferred_element_type=jnp.float32)

    @pl.when(i == 0)
    def _():
        for k in range(split):
            part = slice(k * sub, (k + 1) * sub)
            left = (own_ref[k].astype(jnp.float32) * own_root_ref[:, part]).T
            at_ref[part] = (left * w_ref[...]).astype(jnp.bfloat16)
        q = (p_ref[0, 0, :, :CW].astype(jnp.float32) * r_ref[:, :CW]).T
        q_ref[...] = q
        at_ref[width:] = (q * w_ref[...]).astype(jnp.bfloat16)
        u_ref[...] = jnp.zeros_like(u_ref)

    @pl.when(i < n)
    def _():
        for k in range(split):
            prod = jnp.dot(at_ref[...], p_ref[k, 0], preferred_element_type=jnp.float32) * root(k)
            out_ref[:, k * sub:(k + 1) * sub] = prod[:width].astype(jnp.bfloat16)
            t_ref[:, k * sub:(k + 1) * sub] = prod[width:]

    @pl.when(i < n)
    def _():
        for k in range(split):
            u_ref[...] += spread(k, t_ref[:, k * sub:(k + 1) * sub])

    @pl.when(i == n - 1)
    def _():
        v_ref[...] = (u_ref[...].T * (w_ref[...] * factor)).astype(jnp.bfloat16)

    @pl.when(i >= n)
    def _():
        for k in range(split):
            prod = jnp.dot(v_ref[...], p_ref[k, 0], preferred_element_type=jnp.float32) * root(k)
            u_ref[...] += spread(k, prod)

    @pl.when(i == 2 * n - 1)
    def _():
        x = (q_ref[...] + factor * u_ref[...].T).astype(jnp.bfloat16)
        s_ref[...] = lax.dot_general(
            at_ref[:width], x, (((1,), (1,)), ((), ())), preferred_element_type=jnp.float32)


def chi_and_screen(own, pieces, weight, own_root, coulomb_root):
    split, n, packed, sub = pieces.shape
    width = split * sub
    return pl.pallas_call(
        functools.partial(chi_kernel, n, 8.0 / G),
        grid=(2 * n,),
        out_shape=(
            jax.ShapeDtypeStruct((width, n * split * sub), jnp.bfloat16),
            jax.ShapeDtypeStruct((width, CW), jnp.float32),
        ),
        in_specs=[
            pl.BlockSpec((split, packed, sub), lambda i: (0, 0, 0)),
            pl.BlockSpec((split, 1, packed, sub), lambda i: (0, i % n, 0, 0)),
            pl.BlockSpec((1, packed), lambda i: (0, 0)),
            pl.BlockSpec((1, width), lambda i: (0, 0)),
            pl.BlockSpec((1, split * sub), lambda i: (0, i % n)),
        ],
        out_specs=(
            pl.BlockSpec((width, split * sub), lambda i: (0, jnp.minimum(i, n - 1))),
            pl.BlockSpec((width, CW), lambda i: (0, 0)),
        ),
        scratch_shapes=[
            pltpu.VMEM((width + CW, packed), jnp.bfloat16),
            pltpu.VMEM((CW, packed), jnp.float32),
            pltpu.VMEM((packed, CW), jnp.float32),
            pltpu.VMEM((CW, packed), jnp.bfloat16),
            pltpu.VMEM((CW, width), jnp.float32),
        ],
        compiler_params=pltpu.CompilerParams(vmem_limit_bytes=48 * 1024 * 1024),
    )(own, pieces, weight[None, :], own_root[None, :], coulomb_root[None, :])


def gather_kernel(
    nz, rows_ref, energy_ref, source_ref, out_ref, energies_ref, own_ref,
    all_ref, pick_ref, recv, s_up, s_down, s_y, s_x, s_pair, s_own,
    r_rows, s_rows, s_local, r_energy, s_energy,
):
    g, b = lax.axis_index("grp"), lax.axis_index("blk")
    x, c = g // 2, g % 2
    z, y = b // 2, b % 2
    half = own_ref.shape[1] // 2
    rows = pl.ds(pl.multiple_of(c * half, half), half)
    other_rows = pl.ds(pl.multiple_of((1 - c) * half, half), half)
    to_up, to_down = (g, b + 2), (g, b - 2)
    to_y = (g, z * 2 + 1 - y)
    to_x = ((1 - x) * 2 + c, b)
    to_pair = (x * 2 + 1 - c, b)
    has_up, has_down = z + 1 < nz, z >= 1
    skip_y, own_x = 2 * (1 - x), 2 * x

    def copy(q, bb, sem, to, own=False):
        src = own_ref.at[q, rows] if own else out_ref.at[q, bb, rows]
        return pltpu.make_async_remote_copy(
            src_ref=src, dst_ref=out_ref.at[q, bb, rows], send_sem=sem,
            recv_sem=recv.at[q, bb, c], device_id=to, device_id_type=pl.DeviceIdType.MESH)

    def arrived(q, bb):
        copy(q, bb, s_pair.at[q, bb], to_pair).wait_recv()

    def up(zz, j, own=False):
        return copy(x + j, zz * 2 + y, s_up.at[j, zz], to_up, own)

    def down(zz, j, own=False):
        return copy(x + j, zz * 2 + y, s_down.at[j, zz], to_down, own)

    def over_y(zz, j, own=False):
        return copy(x + j, zz * 2 + y, s_y.at[j, zz], to_y, own)

    def over_x(zz, yy, j):
        return copy(x + j, zz * 2 + yy, s_x.at[j, zz * 2 + yy], to_x)

    def over_pair(q, bb):
        return copy(q, bb, s_pair.at[q, bb], to_pair)

    def takes_y(zz, j):
        return (zz % 2 == 0) | (j != skip_y)

    def other_y_takes_x(zz, j):
        return ((zz % 2 == 0) & (j == own_x)) | ((zz % 2 == 1) & (j != skip_y))

    def when(condition, make, act):
        @pl.when(condition)
        def _():
            getattr(make(), act)()

    def from_z(zz, j, below, valid):
        @pl.when(valid)
        def _():
            q, bb = x + j, zz * 2 + y
            arrived(q, bb)
            if below:
                when(has_up, lambda: up(zz, j), "start")
            else:
                when(has_down, lambda: down(zz, j), "start")
            when(takes_y(zz, j), lambda: over_y(zz, j), "start")
            when(j == own_x, lambda: over_x(zz, y, j), "start")
            over_pair(q, bb).start()

    def from_y(zz, j, valid):
        @pl.when(valid & takes_y(zz, j))
        def _():
            q, bb = x + j, zz * 2 + 1 - y
            arrived(q, bb)
            when(other_y_takes_x(zz, j), lambda: over_x(zz, 1 - y, j), "start")
            over_pair(q, bb).start()

    def from_x(zz, same_y, valid):
        bb = zz * 2 + (y if same_y else 1 - y)

        def take(q):
            arrived(q, bb)
            over_pair(q, bb).start()

        if same_y:
            @pl.when(valid)
            def _():
                take(3 * (1 - x))
        else:
            @pl.when(valid & (zz % 2 == 0))
            def _():
                take(3 * (1 - x))

            @pl.when(valid & (zz % 2 == 1))
            def _():
                take(2 * (1 - x))
                take(2 * (1 - x) + 1)

    def at_distance(d):
        if d == 0:
            return [(z, True, z >= 0)]
        return [(z - d, True, z >= d), (z + d, False, z + d < nz)]

    barrier = pltpu.get_barrier_semaphore()

    def greet(to):
        pl.semaphore_signal(barrier, inc=1, device_id=to, device_id_type=pl.DeviceIdType.MESH)

    for to in (to_y, to_x, to_pair):
        greet(to)
    pl.when(has_up)(lambda: greet(to_up))
    pl.when(has_down)(lambda: greet(to_down))
    peers = 3 + has_up.astype(jnp.int32) + has_down.astype(jnp.int32)
    pl.semaphore_wait(barrier, peers)

    slots, packed, sub = rows_ref.shape[0], own_ref.shape[1], own_ref.shape[2]
    g_x, g_pair = (1 - x) * 2 + c, x * 2 + 1 - c
    g_far = (1 - x) * 2 + 1 - c

    def span(k):
        return pl.ds(pl.multiple_of(k * slots, slots), slots)

    def order(j):
        return jnp.where(j < 3, x + j, 3 * (1 - x))

    def rows_to(q, way, to, who):
        dst = all_ref.at[q, span(who)]
        columns = pl.ds(pl.multiple_of(q * sub, sub), sub)
        return pltpu.make_async_remote_copy(
            src_ref=dst if way == 2 else rows_ref.at[:, columns], dst_ref=dst,
            send_sem=s_rows.at[way, q], recv_sem=r_rows.at[q, who], device_id=to,
            device_id_type=pl.DeviceIdType.MESH)

    def rows_local(q):
        columns = pl.ds(pl.multiple_of(q * sub, sub), sub)
        return pltpu.make_async_copy(rows_ref.at[:, columns], all_ref.at[q, span(g)], s_local.at[q])

    def energy_to(way, to, who):
        return pltpu.make_async_remote_copy(
            src_ref=energies_ref.at[who] if way == 2 else energy_ref.at[0],
            dst_ref=energies_ref.at[who], send_sem=s_energy.at[way], recv_sem=r_energy.at[who],
            device_id=to, device_id_type=pl.DeviceIdType.MESH)

    for j in range(4):
        q = order(j)
        rows_to(q, 0, to_x, g).start()
        rows_to(q, 1, to_pair, g).start()
        rows_local(q).start()
    energy_to(0, to_x, g).start()
    energy_to(1, to_pair, g).start()
    keep_energy = pltpu.make_async_copy(energy_ref.at[0], energies_ref.at[g], s_local.at[4])
    keep_energy.start()

    @pl.loop(0, packed // 128)
    def _(k):
        part = pl.ds(pl.multiple_of(k * 128, 128), 128)
        at = lax.broadcasted_iota(jnp.int32, (128, pick_ref.shape[1]), 1)
        pick_ref[part] = (source_ref[part] == at).astype(jnp.float32).astype(jnp.bfloat16)

    def keep(q):
        return pltpu.make_async_copy(own_ref.at[q], out_ref.at[q, b], s_own.at[q])

    @pl.loop(0, 4)
    def _(j):
        q = order(j)
        rows_to(q, 0, to_x, g_x).wait_recv()
        rows_to(q, 2, to_pair, g_x).start()
        rows_local(q).wait()
        rows_to(q, 1, to_pair, g_pair).wait_recv()
        rows_to(q, 2, to_pair, g_far).wait_recv()
        own_ref[q] = jnp.dot(
            pick_ref[...], all_ref[q], preferred_element_type=jnp.float32).astype(jnp.bfloat16)
        carried = j < 3
        when(carried & has_up, lambda: up(z, j, True), "start")
        when(carried & has_down, lambda: down(z, j, True), "start")
        when(carried & takes_y(z, j), lambda: over_y(z, j, True), "start")
        keep(q).start()

    energy_to(0, to_x, g_x).wait_recv()
    energy_to(2, to_pair, g_x).start()

    for s in range(nz + 2):
        for j in range(3):
            if 1 <= s + 1 < nz:
                for zz, below, valid in at_distance(s + 1):
                    from_z(zz, j, below, valid)
            if s < nz:
                for zz, _, valid in at_distance(s):
                    from_y(zz, j, valid)
        if 2 <= s <= nz:
            for zz, _, valid in at_distance(s - 1):
                from_x(zz, True, valid)
        if s >= 2:
            for zz, _, valid in at_distance(s - 2):
                from_x(zz, False, valid)

    def from_pair(q, bb):
        pltpu.make_async_remote_copy(
            src_ref=out_ref.at[q, bb, other_rows], dst_ref=out_ref.at[q, bb, other_rows],
            send_sem=s_pair.at[q, bb], recv_sem=recv.at[q, bb, 1 - c],
            device_id=to_pair, device_id_type=pl.DeviceIdType.MESH).wait_recv()
        over_pair(q, bb).wait_send()

    energy_to(1, to_pair, g_pair).wait_recv()
    energy_to(2, to_pair, g_far).wait_recv()
    energy_to(0, to_x, g).wait_send()
    energy_to(1, to_pair, g).wait_send()
    energy_to(2, to_pair, g_x).wait_send()
    keep_energy.wait()
    for j in range(4):
        q = order(j)
        rows_to(q, 0, to_x, g).wait_send()
        rows_to(q, 1, to_pair, g).wait_send()
        rows_to(q, 2, to_pair, g_x).wait_send()
        keep(q).wait()
    for j in range(3):
        when(has_up, lambda: up(z, j, True), "wait_send")
        when(has_down, lambda: down(z, j, True), "wait_send")
        when(takes_y(z, j), lambda: over_y(z, j, True), "wait_send")
    for d in range(nz):
        for zz, below, valid in at_distance(d):
            for j in range(3):
                if d >= 1:
                    if below:
                        when(valid & has_up, lambda: up(zz, j), "wait_send")
                    else:
                        when(valid & has_down, lambda: down(zz, j), "wait_send")
                    when(valid & takes_y(zz, j), lambda: over_y(zz, j), "wait_send")
                    when(valid & (j == own_x), lambda: over_x(zz, y, j), "wait_send")
                when(valid & other_y_takes_x(zz, j), lambda: over_x(zz, 1 - y, j), "wait_send")
            for same_y in (True, False):
                if d >= 1 or not same_y:
                    for q in range(4):
                        pl.when(valid)(
                            lambda q=q: from_pair(q, zz * 2 + (y if same_y else 1 - y)))


def gather_pieces(pair_density, energies, source, blocks, split):
    slots, width = pair_density.shape
    packed = source.shape[0]
    sub, nz = width // split, blocks // 2
    dma = pltpu.SemaphoreType.DMA
    vmem = pl.BlockSpec(memory_space=pltpu.VMEM)
    return pl.pallas_call(
        functools.partial(gather_kernel, nz),
        out_shape=(
            jax.ShapeDtypeStruct((split, blocks, packed, sub), jnp.bfloat16),
            jax.ShapeDtypeStruct((split, 1, slots), jnp.float32),
            jax.ShapeDtypeStruct((split, packed, sub), jnp.bfloat16),
        ),
        in_specs=[vmem, vmem, vmem],
        out_specs=(pl.BlockSpec(memory_space=pl.ANY), vmem, vmem),
        scratch_shapes=[
            pltpu.VMEM((split, split * slots, sub), jnp.bfloat16),
            pltpu.VMEM((packed, split * slots), jnp.bfloat16),
            dma((split, blocks, 2)), dma((3, nz)), dma((3, nz)), dma((3, nz)),
            dma((3, blocks)), dma((split, blocks)), dma((split,)),
            dma((split, split)), dma((3, split)), dma((split + 1,)), dma((split,)), dma((3,)),
        ],
        compiler_params=pltpu.CompilerParams(
            collective_id=0, has_side_effects=True, vmem_limit_bytes=40 * 1024 * 1024),
    )(pair_density, energies[None, None, :], source[:, None])


def body(pair_density, energies, batch_live, coulomb_root):
    slots, width = pair_density.shape
    group_count = lax.axis_size("grp")
    blocks = lax.axis_size("blk")
    total = slots * group_count
    packed = total * 5 // 8
    group_index = lax.axis_index("grp")
    block_index = lax.axis_index("blk")
    own_root = lax.dynamic_slice_in_dim(coulomb_root, block_index * width, width)

    source, used = pack_rows(batch_live, slots, total, packed)
    pieces, all_energy, own = gather_pieces(pair_density, energies, source, blocks, group_count)
    pick = source[:, None] == jnp.arange(total, dtype=jnp.int32)[None, :]
    energy = jnp.sum(jnp.where(pick, jnp.reshape(all_energy, (1, total)), 0.0), axis=1)
    energy = jnp.where(used, energy, 1.0)
    frequency = 0.6 * group_index.astype(jnp.float32)
    weight = -2.0 * energy / (energy * energy + frequency * frequency)
    weight = jnp.where(used, weight, 0.0) * (1.0 / math.sqrt(total))
    polarized, screened = chi_and_screen(own, pieces, weight, own_root, coulomb_root)
    return (polarized[None], screened[None])


def solution(mesh):
    placed = (P("grp", "blk"), P("grp"), P(), P())
    aligned = (
        mesh.shape["grp"] == 4
        and mesh.shape["blk"] % 2 == 0
        and (G // mesh.shape["blk"]) % (LANES * mesh.shape["grp"]) == 0
    )
    return jax.shard_map(
        body if aligned else plain_body,
        mesh=mesh,
        in_specs=placed,
        out_specs=(P("grp", "blk", None), P("grp", "blk", None)),
        check_vma=False,
    )
```

```python
import functools
import math

import jax
import jax.numpy as jnp
from jax import lax
from jax.experimental import pallas as pl
from jax.experimental.pallas import tpu as pltpu
from jax.sharding import PartitionSpec as P

G = 8192
CW = 128
DYSON = 2
LANES = 128


def live_weights(all_energy, batch_live, slots, total_slots, group_ids, frequencies, norm_factor):
    positions = jnp.arange(total_slots, dtype=jnp.int32)
    owner_match = (positions // slots)[:, None] == group_ids[None, :]
    limits = jnp.sum(jnp.where(owner_match, batch_live[None, :], 0), axis=1)
    is_live = (positions % slots < limits).astype(jnp.float32)
    weight = (
        -2.0
        * all_energy[None, :]
        / (all_energy[None, :] * all_energy[None, :] + frequencies[:, None] * frequencies[:, None])
    )
    return weight * is_live[None, :] * norm_factor


def plain_body(pair_density, energies, batch_live, coulomb_root):
    slots = pair_density.shape[0]
    width_own = pair_density.shape[1]
    group_count = lax.axis_size("grp")
    block_count = lax.axis_size("blk")
    total_slots = slots * group_count
    group_index = lax.axis_index("grp")
    block_index = lax.axis_index("blk")
    norm_factor = 1.0 / math.sqrt(total_slots)
    own_root = lax.dynamic_slice_in_dim(coulomb_root, block_index * width_own, width_own)
    group_ids = jnp.arange(group_count, dtype=jnp.int32)
    row_density, all_energy = (
        lax.all_gather(pair_density, "grp", axis=0, tiled=True),
        lax.all_gather(energies.astype(jnp.bfloat16), "grp", axis=0, tiled=True).astype(
            energies.dtype
        ),
    )
    frequencies = 0.6 * jnp.arange(group_count, dtype=jnp.float32)
    weight = live_weights(
        all_energy, batch_live, slots, total_slots, group_ids, frequencies, norm_factor
    )
    scaled = (weight[:, :, None] * row_density.astype(jnp.float32)[None, :, :]).astype(jnp.bfloat16)
    sub_width = width_own // group_count
    my_slice = lax.dynamic_slice_in_dim(row_density, group_index * sub_width, sub_width, 1)
    root_table = jnp.reshape(coulomb_root, (block_count, group_count, sub_width))
    my_roots = jnp.reshape(
        lax.dynamic_index_in_dim(root_table, group_index, 1, keepdims=False), (-1,)
    )
    chi = jnp.einsum(
        "ftc,tk->fck",
        scaled,
        lax.all_gather(my_slice, "blk", axis=1, tiled=True),
        preferred_element_type=jnp.float32,
    )
    quarter = own_root[None, :, None] * chi * my_roots[None, None, :]
    received = lax.all_to_all(
        quarter.astype(jnp.bfloat16), "grp", split_axis=0, concat_axis=0, tiled=True
    )
    received = jnp.reshape(received, (group_count, width_own, block_count, sub_width))
    polarized = jnp.reshape(
        jnp.transpose(received, (1, 2, 0, 3)), (width_own, width_own * block_count)
    )
    lead_blocks = (CW + width_own - 1) // width_own
    lead = quarter[:, :, : lead_blocks * sub_width]
    lead_back = lax.all_to_all(
        lead.astype(jnp.bfloat16), "grp", split_axis=0, concat_axis=0, tiled=True
    ).astype(lead.dtype)
    lead_back = jnp.reshape(lead_back, (group_count, width_own, lead_blocks, sub_width))
    window = jnp.reshape(
        jnp.transpose(lead_back, (1, 2, 0, 3)), (width_own, lead_blocks * width_own)
    )[:, :CW]
    state = window
    for dyson_step in range(DYSON):
        rounded = state.astype(jnp.bfloat16)
        product = jnp.dot(
            polarized,
            lax.all_gather(rounded, "blk", axis=0, tiled=True),
            preferred_element_type=jnp.float32,
        )
        state = window + 8.0 / G * product
    return (polarized[None], state[None])


def pack_rows(batch_live, slots, total, packed):
    ends = jnp.cumsum(batch_live)
    starts = ends - batch_live
    j = jnp.arange(packed, dtype=jnp.int32)
    in_group = (j[:, None] >= starts[None, :]) & (j[:, None] < ends[None, :])
    group_base = jnp.arange(batch_live.shape[0], dtype=jnp.int32) * slots - starts
    source = jnp.sum(jnp.where(in_group, group_base[None, :] + j[:, None], 0), axis=1)
    used = jnp.any(in_group, axis=1)
    source = jnp.where(used, source, -1)
    return source, used


def chi_kernel(
    n, factor, own_ref, p_ref, w_ref, own_root_ref, r_ref, out_ref, s_ref,
    at_ref, q_ref, u_ref, v_ref, t_ref,
):
    i = pl.program_id(0)
    width = at_ref.shape[0] - CW
    split, _, _, sub = p_ref.shape

    def root(k):
        return r_ref[:, k * sub:(k + 1) * sub]

    def spread(k, part):
        part = (part * root(k)).T.astype(jnp.bfloat16)
        return jnp.dot(p_ref[k, 0], part, preferred_element_type=jnp.float32)

    @pl.when(i == 0)
    def _():
        for k in range(split):
            part = slice(k * sub, (k + 1) * sub)
            left = (own_ref[k].astype(jnp.float32) * own_root_ref[:, part]).T
            at_ref[part] = (left * w_ref[...]).astype(jnp.bfloat16)
        q = (p_ref[0, 0, :, :CW].astype(jnp.float32) * r_ref[:, :CW]).T
        q_ref[...] = q
        at_ref[width:] = (q * w_ref[...]).astype(jnp.bfloat16)
        u_ref[...] = jnp.zeros_like(u_ref)

    @pl.when(i < n)
    def _():
        for k in range(split):
            prod = jnp.dot(at_ref[...], p_ref[k, 0], preferred_element_type=jnp.float32) * root(k)
            out_ref[:, k * sub:(k + 1) * sub] = prod[:width].astype(jnp.bfloat16)
            t_ref[:, k * sub:(k + 1) * sub] = prod[width:]

    @pl.when(i < n)
    def _():
        for k in range(split):
            u_ref[...] += spread(k, t_ref[:, k * sub:(k + 1) * sub])

    @pl.when(i == n - 1)
    def _():
        v_ref[...] = (u_ref[...].T * (w_ref[...] * factor)).astype(jnp.bfloat16)

    @pl.when(i >= n)
    def _():
        for k in range(split):
            prod = jnp.dot(v_ref[...], p_ref[k, 0], preferred_element_type=jnp.float32) * root(k)
            u_ref[...] += spread(k, prod)

    @pl.when(i == 2 * n - 1)
    def _():
        x = (q_ref[...] + factor * u_ref[...].T).astype(jnp.bfloat16)
        s_ref[...] = lax.dot_general(
            at_ref[:width], x, (((1,), (1,)), ((), ())), preferred_element_type=jnp.float32)


def chi_and_screen(own, pieces, weight, own_root, coulomb_root):
    split, n, packed, sub = pieces.shape
    width = split * sub
    return pl.pallas_call(
        functools.partial(chi_kernel, n, 8.0 / G),
        grid=(2 * n,),
        out_shape=(
            jax.ShapeDtypeStruct((width, n * split * sub), jnp.bfloat16),
            jax.ShapeDtypeStruct((width, CW), jnp.float32),
        ),
        in_specs=[
            pl.BlockSpec((split, packed, sub), lambda i: (0, 0, 0)),
            pl.BlockSpec((split, 1, packed, sub), lambda i: (0, i % n, 0, 0)),
            pl.BlockSpec((1, packed), lambda i: (0, 0)),
            pl.BlockSpec((1, width), lambda i: (0, 0)),
            pl.BlockSpec((1, split * sub), lambda i: (0, i % n)),
        ],
        out_specs=(
            pl.BlockSpec((width, split * sub), lambda i: (0, jnp.minimum(i, n - 1))),
            pl.BlockSpec((width, CW), lambda i: (0, 0)),
        ),
        scratch_shapes=[
            pltpu.VMEM((width + CW, packed), jnp.bfloat16),
            pltpu.VMEM((CW, packed), jnp.float32),
            pltpu.VMEM((packed, CW), jnp.float32),
            pltpu.VMEM((CW, packed), jnp.bfloat16),
            pltpu.VMEM((CW, width), jnp.float32),
        ],
        compiler_params=pltpu.CompilerParams(vmem_limit_bytes=48 * 1024 * 1024),
    )(own, pieces, weight[None, :], own_root[None, :], coulomb_root[None, :])


def gather_kernel(
    nz, rows_ref, energy_ref, source_ref, out_ref, energies_ref, own_ref,
    all_ref, pick_ref, recv, s_up, s_down, s_y, s_x, s_pair, s_own,
    r_rows, s_rows, s_local, r_energy, s_energy,
):
    g, b = lax.axis_index("grp"), lax.axis_index("blk")
    x, c = g // 2, g % 2
    z, y = b // 2, b % 2
    half = own_ref.shape[1] // 2
    rows = pl.ds(pl.multiple_of(c * half, half), half)
    other_rows = pl.ds(pl.multiple_of((1 - c) * half, half), half)
    to_up, to_down = (g, b + 2), (g, b - 2)
    to_y = (g, z * 2 + 1 - y)
    to_x = ((1 - x) * 2 + c, b)
    to_pair = (x * 2 + 1 - c, b)
    has_up, has_down = z + 1 < nz, z >= 1
    own_x = 2 * x

    def copy(q, bb, sem, to, own=False):
        src = own_ref.at[q, rows] if own else out_ref.at[q, bb, rows]
        return pltpu.make_async_remote_copy(
            src_ref=src, dst_ref=out_ref.at[q, bb, rows], send_sem=sem,
            recv_sem=recv.at[q, bb, c], device_id=to, device_id_type=pl.DeviceIdType.MESH)

    def arrived(q, bb):
        copy(q, bb, s_pair.at[q, bb], to_pair).wait_recv()

    def up(zz, j, own=False):
        return copy(x + j, zz * 2 + y, s_up.at[j, zz], to_up, own)

    def down(zz, j, own=False):
        return copy(x + j, zz * 2 + y, s_down.at[j, zz], to_down, own)

    def over_y(zz, j, own=False):
        return copy(x + j, zz * 2 + y, s_y.at[j, zz], to_y, own)

    def over_x(zz, yy, j):
        return copy(x + j, zz * 2 + yy, s_x.at[j, zz * 2 + yy], to_x)

    def over_pair(q, bb):
        return copy(q, bb, s_pair.at[q, bb], to_pair)

    def takes_y(zz, j):
        return zz >= 0

    def other_y_takes_x(zz, j):
        return (zz >= 0) & (j == own_x)

    def when(condition, make, act):
        @pl.when(condition)
        def _():
            getattr(make(), act)()

    def from_z(zz, j, below, valid):
        @pl.when(valid)
        def _():
            q, bb = x + j, zz * 2 + y
            arrived(q, bb)
            if below:
                when(has_up, lambda: up(zz, j), "start")
            else:
                when(has_down, lambda: down(zz, j), "start")
            when(takes_y(zz, j), lambda: over_y(zz, j), "start")
            when(j == own_x, lambda: over_x(zz, y, j), "start")
            over_pair(q, bb).start()

    def from_y(zz, j, valid):
        @pl.when(valid & takes_y(zz, j))
        def _():
            q, bb = x + j, zz * 2 + 1 - y
            arrived(q, bb)
            when(other_y_takes_x(zz, j), lambda: over_x(zz, 1 - y, j), "start")
            over_pair(q, bb).start()

    def from_x(zz, same_y, valid):
        bb = zz * 2 + (y if same_y else 1 - y)

        def take(q):
            arrived(q, bb)
            over_pair(q, bb).start()

        @pl.when(valid)
        def _():
            take(3 * (1 - x))

    def at_distance(d):
        if d == 0:
            return [(z, True, z >= 0)]
        return [(z - d, True, z >= d), (z + d, False, z + d < nz)]

    barrier = pltpu.get_barrier_semaphore()

    def greet(to):
        pl.semaphore_signal(barrier, inc=1, device_id=to, device_id_type=pl.DeviceIdType.MESH)

    for to in (to_y, to_x, to_pair):
        greet(to)
    pl.when(has_up)(lambda: greet(to_up))
    pl.when(has_down)(lambda: greet(to_down))
    peers = 3 + has_up.astype(jnp.int32) + has_down.astype(jnp.int32)
    pl.semaphore_wait(barrier, peers)

    slots, packed, sub = rows_ref.shape[0], own_ref.shape[1], own_ref.shape[2]
    g_x, g_pair = (1 - x) * 2 + c, x * 2 + 1 - c
    g_far = (1 - x) * 2 + 1 - c

    def span(k):
        return pl.ds(pl.multiple_of(k * slots, slots), slots)

    def order(j):
        return jnp.where(j < 3, x + j, 3 * (1 - x))

    def rows_to(q, way, to, who):
        dst = all_ref.at[q, span(who)]
        columns = pl.ds(pl.multiple_of(q * sub, sub), sub)
        return pltpu.make_async_remote_copy(
            src_ref=dst if way == 2 else rows_ref.at[:, columns], dst_ref=dst,
            send_sem=s_rows.at[way, q], recv_sem=r_rows.at[q, who], device_id=to,
            device_id_type=pl.DeviceIdType.MESH)

    def rows_local(q):
        columns = pl.ds(pl.multiple_of(q * sub, sub), sub)
        return pltpu.make_async_copy(rows_ref.at[:, columns], all_ref.at[q, span(g)], s_local.at[q])

    def energy_to(way, to, who):
        return pltpu.make_async_remote_copy(
            src_ref=energies_ref.at[who] if way == 2 else energy_ref.at[0],
            dst_ref=energies_ref.at[who], send_sem=s_energy.at[way], recv_sem=r_energy.at[who],
            device_id=to, device_id_type=pl.DeviceIdType.MESH)

    for j in range(4):
        q = order(j)
        rows_to(q, 0, to_x, g).start()
        rows_to(q, 1, to_pair, g).start()
        rows_local(q).start()
    energy_to(0, to_x, g).start()
    energy_to(1, to_pair, g).start()
    keep_energy = pltpu.make_async_copy(energy_ref.at[0], energies_ref.at[g], s_local.at[4])
    keep_energy.start()

    @pl.loop(0, packed // 128)
    def _(k):
        part = pl.ds(pl.multiple_of(k * 128, 128), 128)
        at = lax.broadcasted_iota(jnp.int32, (128, pick_ref.shape[1]), 1)
        pick_ref[part] = (source_ref[part] == at).astype(jnp.float32).astype(jnp.bfloat16)

    def keep(q):
        return pltpu.make_async_copy(own_ref.at[q], out_ref.at[q, b], s_own.at[q])

    @pl.loop(0, 4)
    def _(j):
        q = order(j)
        rows_to(q, 0, to_x, g_x).wait_recv()
        rows_to(q, 2, to_pair, g_x).start()
        rows_local(q).wait()
        rows_to(q, 1, to_pair, g_pair).wait_recv()
        rows_to(q, 2, to_pair, g_far).wait_recv()
        own_ref[q] = jnp.dot(
            pick_ref[...], all_ref[q], preferred_element_type=jnp.float32).astype(jnp.bfloat16)
        carried = j < 3
        when(carried & has_up, lambda: up(z, j, True), "start")
        when(carried & has_down, lambda: down(z, j, True), "start")
        when(carried & takes_y(z, j), lambda: over_y(z, j, True), "start")
        keep(q).start()

    energy_to(0, to_x, g_x).wait_recv()
    energy_to(2, to_pair, g_x).start()

    for s in range(nz + 1):
        for j in range(3):
            if 1 <= s + 1 < nz:
                for zz, below, valid in at_distance(s + 1):
                    from_z(zz, j, below, valid)
            if s < nz:
                for zz, _, valid in at_distance(s):
                    from_y(zz, j, valid)
        if 1 <= s < nz:
            for zz, _, valid in at_distance(s):
                from_x(zz, True, valid)
        if s >= 1:
            for zz, _, valid in at_distance(s - 1):
                from_x(zz, False, valid)

    def from_pair(q, bb):
        pltpu.make_async_remote_copy(
            src_ref=out_ref.at[q, bb, other_rows], dst_ref=out_ref.at[q, bb, other_rows],
            send_sem=s_pair.at[q, bb], recv_sem=recv.at[q, bb, 1 - c],
            device_id=to_pair, device_id_type=pl.DeviceIdType.MESH).wait_recv()
        over_pair(q, bb).wait_send()

    energy_to(1, to_pair, g_pair).wait_recv()
    energy_to(2, to_pair, g_far).wait_recv()
    energy_to(0, to_x, g).wait_send()
    energy_to(1, to_pair, g).wait_send()
    energy_to(2, to_pair, g_x).wait_send()
    keep_energy.wait()
    for j in range(4):
        q = order(j)
        rows_to(q, 0, to_x, g).wait_send()
        rows_to(q, 1, to_pair, g).wait_send()
        rows_to(q, 2, to_pair, g_x).wait_send()
        keep(q).wait()
    for j in range(3):
        when(has_up, lambda: up(z, j, True), "wait_send")
        when(has_down, lambda: down(z, j, True), "wait_send")
        when(takes_y(z, j), lambda: over_y(z, j, True), "wait_send")
    for d in range(nz):
        for zz, below, valid in at_distance(d):
            for j in range(3):
                if d >= 1:
                    if below:
                        when(valid & has_up, lambda: up(zz, j), "wait_send")
                    else:
                        when(valid & has_down, lambda: down(zz, j), "wait_send")
                    when(valid & takes_y(zz, j), lambda: over_y(zz, j), "wait_send")
                    when(valid & (j == own_x), lambda: over_x(zz, y, j), "wait_send")
                when(valid & other_y_takes_x(zz, j), lambda: over_x(zz, 1 - y, j), "wait_send")
            for same_y in (True, False):
                if d >= 1 or not same_y:
                    for q in range(4):
                        pl.when(valid)(
                            lambda q=q: from_pair(q, zz * 2 + (y if same_y else 1 - y)))


def gather_pieces(pair_density, energies, source, blocks, split):
    slots, width = pair_density.shape
    packed = source.shape[0]
    sub, nz = width // split, blocks // 2
    dma = pltpu.SemaphoreType.DMA
    vmem = pl.BlockSpec(memory_space=pltpu.VMEM)
    return pl.pallas_call(
        functools.partial(gather_kernel, nz),
        out_shape=(
            jax.ShapeDtypeStruct((split, blocks, packed, sub), jnp.bfloat16),
            jax.ShapeDtypeStruct((split, 1, slots), jnp.float32),
            jax.ShapeDtypeStruct((split, packed, sub), jnp.bfloat16),
        ),
        in_specs=[vmem, vmem, vmem],
        out_specs=(pl.BlockSpec(memory_space=pl.ANY), vmem, vmem),
        scratch_shapes=[
            pltpu.VMEM((split, split * slots, sub), jnp.bfloat16),
            pltpu.VMEM((packed, split * slots), jnp.bfloat16),
            dma((split, blocks, 2)), dma((3, nz)), dma((3, nz)), dma((3, nz)),
            dma((3, blocks)), dma((split, blocks)), dma((split,)),
            dma((split, split)), dma((3, split)), dma((split + 1,)), dma((split,)), dma((3,)),
        ],
        compiler_params=pltpu.CompilerParams(
            collective_id=0, has_side_effects=True, vmem_limit_bytes=40 * 1024 * 1024),
    )(pair_density, energies[None, None, :], source[:, None])


def body(pair_density, energies, batch_live, coulomb_root):
    slots, width = pair_density.shape
    group_count = lax.axis_size("grp")
    blocks = lax.axis_size("blk")
    total = slots * group_count
    packed = total * 5 // 8
    group_index = lax.axis_index("grp")
    block_index = lax.axis_index("blk")
    own_root = lax.dynamic_slice_in_dim(coulomb_root, block_index * width, width)

    source, used = pack_rows(batch_live, slots, total, packed)
    pieces, all_energy, own = gather_pieces(pair_density, energies, source, blocks, group_count)
    pick = source[:, None] == jnp.arange(total, dtype=jnp.int32)[None, :]
    energy = jnp.sum(jnp.where(pick, jnp.reshape(all_energy, (1, total)), 0.0), axis=1)
    energy = jnp.where(used, energy, 1.0)
    frequency = 0.6 * group_index.astype(jnp.float32)
    weight = -2.0 * energy / (energy * energy + frequency * frequency)
    weight = jnp.where(used, weight, 0.0) * (1.0 / math.sqrt(total))
    polarized, screened = chi_and_screen(own, pieces, weight, own_root, coulomb_root)
    return (polarized[None], screened[None])


def solution(mesh):
    placed = (P("grp", "blk"), P("grp"), P(), P())
    aligned = (
        mesh.shape["grp"] == 4
        and mesh.shape["blk"] % 2 == 0
        and (G // mesh.shape["blk"]) % (LANES * mesh.shape["grp"]) == 0
    )
    return jax.shard_map(
        body if aligned else plain_body,
        mesh=mesh,
        in_specs=placed,
        out_specs=(P("grp", "blk", None), P("grp", "blk", None)),
        check_vma=False,
    )
```
